32 devices in a mesh: groups: 2 (over x), hist: 16 (over z, y, core).
Axes of the slice: x: 2, y: 2, z: 4, core: 2. Of those that a mesh axis runs over, the one named last changes fastest.
Arguments:
- history: bfloat16 [16384, 1024], P(('groups', 'hist')), parts along dimension 0, may hold values from -6 to 6
- candidates: bfloat16 [512, 1024], P(('groups', 'hist')), parts along dimension 0, may hold values from -6 to 6
- hist_length: int32 [2], P('groups'), parts along dimension 0, may hold values from 4096 to 8192
- visible: int32 [512], P(('groups', 'hist')), parts along dimension 0, may hold values from 1 to 8192
- w_proj: bfloat16 [1024, 4096], replicated, may hold values from -0.1875 to 0.1875
- w_out: bfloat16 [1024, 1024], replicated, may hold values from -0.1875 to 0.1875
Outputs:
- scored: bfloat16 [512, 1024], P(('groups', 'hist')), parts along dimension 0
The draws below stay inside these ranges and needn't reach their ends.
There are 2 independent parts, one for each index of `groups`. The reference program is written for one: setup_inputs(seed, part) draws one part's arguments, and reference() takes and returns one part's arrays. A program takes and returns all parts, laid end to end along the dimension named above; an argument that names none is the same for every part. Nothing has to cross between parts.
All inputs are finite; a program needn't handle non-finite values.
Results may differ from the reference program's by a relative error of at most 0.0022.
The reference program's roundings to bfloat16 on the way (of `hist_norm`, `hist_kv`, `cand_norm`, `proj`, `weight` and `mixed`) count: a program that leaves them out, or rounds other values in their place, can miss the bound.
Values may be sent and summed in bfloat16 or wider, within the bound.
No kernel may reach another device: no remote copies, remote signals or barrier semaphores. Data moves between devices by JAX's collectives and lax.ppermute only.
A program may use at most 64 MiB of HBM per device.

```python
import jax
import jax.numpy as jnp
from jax import lax

D = 1024
HEADS = 8
C_DEV = 16
HIST = 8192
NC = 256


def set_ends(values, own_key, low, high):
    longest = values.shape.index(max(values.shape))
    spots = []
    for shift in (0, 1):
        where = [jax.random.randint(jax.random.fold_in(own_key, axis), (), 0, length) for axis, length in enumerate(values.shape)]
        where[longest] = (where[longest] + shift) % values.shape[longest]
        spots.append(tuple(where))
    return values.at[spots[0]].set(low).at[spots[1]].set(high)


def steps_of(stream_key, shape, shards, low, top_value):
    factor_of = 1.0
    for dim, parts in shards:
        steps = jax.random.uniform(jax.random.fold_in(jax.random.fold_in(stream_key, 6), dim), (parts,), jnp.float32, low / len(shards), top_value / len(shards))
        factor_of = factor_of * jnp.repeat(jnp.exp(steps), shape[dim] // parts).reshape((-1,) + (1,) * (len(shape) - 1 - dim))
    return factor_of


def bell_draw(rng, extent, scale, bound, cuts=(), held_as=jnp.bfloat16):
    level = steps_of(rng, extent, cuts, -0.22, 0.18) if cuts else 1.0
    array = jax.random.normal(rng, extent, jnp.float32) * scale * level
    return jnp.minimum(jnp.maximum(array, -bound), bound).astype(held_as)


def setup_inputs(seed: int = 0, part: int = 0) -> dict:
    streams_of = jax.random.split(jax.random.key(seed), 7)
    part_keys = jax.random.split(jax.random.fold_in(streams_of[6], part), 7)
    history = bell_draw(part_keys[0], (HIST, D), 1.0, 6.0, ((0, 16),))
    candidates = bell_draw(part_keys[1], (NC, D), 1.0, 6.0, ((0, 16),))
    hist_length = jax.random.randint(part_keys[2], (1,), HIST // 2, HIST + 1).astype(jnp.int32)
    visible = set_ends(jax.random.randint(part_keys[3], (NC,), 1, HIST + 1), jax.random.fold_in(part_keys[3], 1), 1, HIST).astype(jnp.int32)
    w_proj = bell_draw(streams_of[4], (D, 4 * D), D ** -0.5, 0.1875)
    w_out = bell_draw(streams_of[5], (D, D), D ** -0.5, 0.1875)
    return dict(history=history, candidates=candidates, hist_length=hist_length, visible=visible, w_proj=w_proj, w_out=w_out)


EPS = 1e-06

def layer_norm(rows):
    rows = rows.astype(jnp.float32)
    centred = rows - lax.optimization_barrier(jnp.mean(rows, axis=-1, keepdims=True))
    spread = lax.optimization_barrier(jnp.mean(centred * centred, axis=-1, keepdims=True))
    return centred * lax.rsqrt(spread + EPS)

def attend(query, limit, keys, values):
    rows = query.shape[0]
    n_keys = keys.shape[0]
    head_size = query.shape[1] // HEADS
    q_f = query.astype(jnp.float32).reshape(rows, HEADS, head_size)
    k_f = keys.astype(jnp.float32).reshape(n_keys, HEADS, head_size)
    v_f = values.astype(jnp.float32).reshape(n_keys, HEADS, head_size)
    scores = jnp.einsum('rhd,khd->hrk', q_f, k_f, precision=lax.Precision.HIGHEST)
    position = jnp.arange(n_keys, dtype=jnp.int32)
    seen = (position[None, :] < limit[:, None]).astype(jnp.float32)
    count = (limit + 1).astype(jnp.float32)
    weight = jax.nn.silu(scores * head_size ** (-0.5)) * seen[None] / count[None, :, None]
    weight = weight.astype(jnp.bfloat16).astype(jnp.float32)
    out = jnp.einsum('hrk,khd->rhd', weight, v_f, precision=lax.Precision.HIGHEST)
    return out.reshape(rows, -1)

def reference(history, candidates, hist_length, visible, w_proj, w_out):
    width = w_out.shape[0]
    head_size = width // HEADS
    hist_norm = layer_norm(history).astype(jnp.bfloat16)
    hist_kv = jax.nn.silu(jnp.dot(hist_norm, w_proj[:, 2 * width:], preferred_element_type=jnp.float32)).astype(jnp.bfloat16)
    keys_all = hist_kv[:, :width]
    values_all = hist_kv[:, width:]
    cand_norm = layer_norm(candidates).astype(jnp.bfloat16)
    proj = jax.nn.silu(jnp.dot(cand_norm, w_proj, preferred_element_type=jnp.float32)).astype(jnp.bfloat16)
    gate = proj[:, :width]
    query = proj[:, width:2 * width]
    self_key = proj[:, 2 * width:3 * width]
    self_value = proj[:, 3 * width:]
    limit = jnp.minimum(visible, hist_length[0]).astype(jnp.int32)
    count = (limit + 1).astype(jnp.float32)
    rows_all = query.shape[0]
    blocks = rows_all // C_DEV
    query_blocks = query.reshape(blocks, C_DEV, width)
    limit_blocks = limit.reshape(blocks, C_DEV)

    def one_block(pair):
        return attend(pair[0], pair[1], keys_all, values_all)
    attended = lax.map(one_block, (query_blocks, limit_blocks)).reshape(rows_all, width)
    self_scores = (query.astype(jnp.float32) * self_key.astype(jnp.float32)).reshape(rows_all, HEADS, head_size).sum(-1)
    self_weight = (jax.nn.silu(self_scores * head_size ** (-0.5)) / count[:, None]).astype(jnp.bfloat16).astype(jnp.float32)
    self_term = (self_weight[:, :, None] * self_value.astype(jnp.float32).reshape(rows_all, HEADS, head_size)).reshape(rows_all, width)
    attended = attended + self_term
    mixed = (layer_norm(attended) * gate.astype(jnp.float32)).astype(jnp.bfloat16)
    result = candidates.astype(jnp.float32) + jnp.dot(mixed, w_out, preferred_element_type=jnp.float32)
    return result.astype(jnp.bfloat16)
```

```python
import jax
import jax.numpy as jnp
from jax import lax
from jax.experimental import pallas as pl
from jax.experimental.pallas import tpu as pltpu
from jax.sharding import PartitionSpec as P


HEADS = 8
EPS = 1e-06
EXTRA = 128
STEPS = 32000.0
GRANT = 8 * 1024 * 1024
PARAMS = pltpu.CompilerParams(vmem_limit_bytes=GRANT)


def swapped(shard, axis, mask):
    size = lax.axis_size(axis)
    return lax.ppermute(shard, axis, [(i, i ^ mask) for i in range(size)])


def norm(rows):
    centred = rows - jnp.mean(rows, axis=-1, keepdims=True)
    spread = jnp.mean(centred * centred, axis=-1, keepdims=True)
    return centred * lax.rsqrt(spread + EPS)


def silu(x):
    half = x * 0.5
    return half + half * jnp.tanh(half)


def whole():
    return pl.BlockSpec(memory_space=pltpu.VMEM)


def encode(rows, out_ref):
    count, width = rows.shape
    top = jnp.max(jnp.abs(rows), axis=-1, keepdims=True)
    exponent = jnp.ceil(jnp.log2(jnp.maximum(top, 1e-30)))
    code = jnp.round(rows * (STEPS * jnp.exp2(-exponent)))
    out_ref[:, :width] = code.astype(jnp.int32).astype(jnp.int16)
    out_ref[:, width:] = (
        jnp.broadcast_to(exponent, (count, EXTRA)).astype(jnp.int32).astype(jnp.int16)
    )


def decode(code, width):
    code = code.astype(jnp.int32).astype(jnp.float32)
    return code[:, :width] * (jnp.exp2(code[:, width : width + 1]) * (1 / STEPS))


def pack_kernel(length_ref, cand_ref, visible_ref, out_ref):
    rows, width = cand_ref.shape
    out_ref[:, :width] = norm(cand_ref[...].astype(jnp.float32)).astype(jnp.bfloat16)
    seen = jnp.broadcast_to(visible_ref[...], (rows, rows))
    diagonal = lax.broadcasted_iota(jnp.int32, (rows, rows), 0) == lax.broadcasted_iota(
        jnp.int32, (rows, rows), 1
    )
    limit = jnp.minimum(seen, length_ref[0]).astype(jnp.float32)
    limit = jnp.sum(jnp.where(diagonal, limit, 0.0), axis=1, keepdims=True)
    high = jnp.floor(limit * (1 / 256))
    low = limit - high * 256
    lane = lax.broadcasted_iota(jnp.int32, (rows, EXTRA), 1)
    out_ref[:, width:] = jnp.where(lane == 0, high, low).astype(jnp.bfloat16)


def pack(candidates, hist_length, visible):
    rows, width = candidates.shape
    return pl.pallas_call(
        pack_kernel,
        out_shape=jax.ShapeDtypeStruct((rows, width + EXTRA), jnp.bfloat16),
        in_specs=[pl.BlockSpec(memory_space=pltpu.SMEM), whole(), whole()],
        out_specs=whole(),
        compiler_params=PARAMS,
        name="pack",
    )(hist_length, candidates, visible.reshape(1, rows))


def limits_of(packed, width):
    high = packed[:, width : width + 1].astype(jnp.float32)
    low = packed[:, width + 1 : width + 2].astype(jnp.float32)
    return high * 256 + low


def project_kernel(first, tile, hist_ref, packed_ref, w_ref, out_ref, self_ref, rows_ref):
    n_keys, width = hist_ref.shape
    rows_ref[:n_keys] = norm(hist_ref[...].astype(jnp.float32)).astype(jnp.bfloat16)
    rows_ref[n_keys:] = packed_ref[:, :width]
    for start in range(0, width, tile):
        made = silu(
            jnp.dot(
                rows_ref[...],
                w_ref[:, first + start : first + start + tile],
                preferred_element_type=jnp.float32,
            )
        ).astype(jnp.bfloat16)
        out_ref[:, start : start + tile] = made[:n_keys]
        self_ref[:, start : start + tile] = made[n_keys:]


def project(history, packed, w_proj, first):
    n_keys, width = history.shape
    rows = packed.shape[0]
    tile = min(256, width)

    def body(*refs):
        project_kernel(first, tile, *refs)

    return pl.pallas_call(
        body,
        out_shape=(
            jax.ShapeDtypeStruct((n_keys, width), jnp.bfloat16),
            jax.ShapeDtypeStruct((rows, width), jnp.bfloat16),
        ),
        in_specs=[whole()] * 3,
        out_specs=(whole(), whole()),
        scratch_shapes=[pltpu.VMEM((n_keys + rows, width), jnp.bfloat16)],
        cost_estimate=pl.CostEstimate(
            flops=2 * (n_keys + rows) * width * width,
            bytes_accessed=4 * width * width,
            transcendentals=(n_keys + rows) * width,
        ),
        compiler_params=PARAMS,
    )(history, packed, w_proj)


def attend_kernel(heads, coded, base_ref, packed_ref, w_ref, k0, v0, k1, v1, out_ref, acc_ref):
    n_keys, width = k0.shape
    size = width // heads
    rows = packed_ref.shape[0]
    limit = limits_of(packed_ref[...], width)
    inverse = 1.0 / (limit + 1.0)
    position = lax.broadcasted_iota(jnp.int32, (rows, n_keys), 1).astype(jnp.float32)
    share = []
    for side in range(2):
        base = base_ref[side].astype(jnp.float32)
        share.append(jnp.where(position + base < limit, inverse, 0.0))
    pair = 2 * size
    for start in range(0, width, pair):
        query = silu(
            jnp.dot(
                packed_ref[:, :width],
                w_ref[:, width + start : width + start + pair],
                preferred_element_type=jnp.float32,
            )
        ).astype(jnp.bfloat16)
        for sub in range(0, pair, size):
            cols = slice(start + sub, start + sub + size)
            total = None
            for side, (k, v) in enumerate(((k0, v0), (k1, v1))):
                scores = lax.dot_general(
                    query[:, sub : sub + size],
                    k[:, cols],
                    (((1,), (1,)), ((), ())),
                    preferred_element_type=jnp.float32,
                )
                weight = (silu(scores * size ** (-0.5)) * share[side]).astype(jnp.bfloat16)
                part = jnp.dot(weight, v[:, cols], preferred_element_type=jnp.float32)
                total = part if total is None else total + part
            acc_ref[:, cols] = total
    made = acc_ref[...]
    made = made - jnp.mean(made, axis=-1, keepdims=True)
    if coded:
        encode(made, out_ref)
    else:
        out_ref[...] = made


def attend(bases, packed, w_proj, k0, v0, k1, v1, heads, coded):
    rows = packed.shape[0]
    n_keys, width = k0.shape

    def body(*refs):
        attend_kernel(heads, coded, *refs)

    return pl.pallas_call(
        body,
        out_shape=jax.ShapeDtypeStruct((rows, width + EXTRA), jnp.int16)
        if coded
        else jax.ShapeDtypeStruct((rows, width), jnp.float32),
        in_specs=[pl.BlockSpec(memory_space=pltpu.SMEM)] + [whole()] * 6,
        out_specs=whole(),
        scratch_shapes=[pltpu.VMEM((rows, width), jnp.float32)],
        cost_estimate=pl.CostEstimate(
            flops=2 * rows * width * (width + 4 * n_keys),
            bytes_accessed=4 * width * width,
            transcendentals=rows * width * 2 * n_keys // 128,
        ),
        compiler_params=PARAMS,
    )(bases, packed, w_proj, k0, v0, k1, v1)


def own_kernel(heads, packed_ref, w_ref, key_ref, value_ref, gate_ref, term_ref):
    _, width = key_ref.shape
    size = width // heads
    both = silu(
        jnp.dot(
            packed_ref[:, :width], w_ref[:, : 2 * width], preferred_element_type=jnp.float32
        )
    ).astype(jnp.bfloat16)
    gate_ref[...] = both[:, :width]
    query = both[:, width:].astype(jnp.float32)
    inverse = 1.0 / (limits_of(packed_ref[...], width) + 1.0)
    products = query * key_ref[...].astype(jnp.float32)
    for head in range(heads):
        cols = slice(head * size, (head + 1) * size)
        score = jnp.sum(products[:, cols], axis=-1, keepdims=True)
        weight = (silu(score * size ** (-0.5)) * inverse).astype(jnp.bfloat16)
        term_ref[:, cols] = weight.astype(jnp.float32) * value_ref[:, cols].astype(jnp.float32)


def own(packed, w_proj, self_key, self_value, heads):
    rows, width = self_key.shape

    def body(*refs):
        own_kernel(heads, *refs)

    return pl.pallas_call(
        body,
        out_shape=(
            jax.ShapeDtypeStruct((rows, width), jnp.bfloat16),
            jax.ShapeDtypeStruct((rows, width), jnp.float32),
        ),
        in_specs=[whole()] * 4,
        out_specs=(whole(), whole()),
        cost_estimate=pl.CostEstimate(
            flops=4 * rows * width * width,
            bytes_accessed=4 * width * width,
            transcendentals=rows * width,
        ),
        compiler_params=PARAMS,
        name="own",
    )(packed, w_proj, self_key, self_value)


def finish_kernel(cand_ref, kept_ref, got_ref, term_ref, gate_ref, w_ref, out_ref):
    attended = kept_ref[...] + decode(got_ref[...], kept_ref.shape[1]) + term_ref[...]
    mixed = (norm(attended) * gate_ref[...].astype(jnp.float32)).astype(jnp.bfloat16)
    out_ref[...] = (
        cand_ref[...].astype(jnp.float32)
        + jnp.dot(mixed, w_ref[...], preferred_element_type=jnp.float32)
    ).astype(jnp.bfloat16)


def finish(candidates, kept, got, term, gate, w_out):
    return pl.pallas_call(
        finish_kernel,
        out_shape=jax.ShapeDtypeStruct(candidates.shape, jnp.bfloat16),
        in_specs=[whole()] * 6,
        out_specs=whole(),
        compiler_params=PARAMS,
        name="finish",
    )(candidates, kept, got, term, gate, w_out)


def combine_kernel(kept_ref, got_ref, sent_ref, out_ref):
    half, width = out_ref.shape
    encode(kept_ref[half:] + decode(got_ref[half:], width), sent_ref)
    out_ref[...] = kept_ref[:half] + decode(got_ref[:half], width)


def combine(kept, got):
    half, width = kept.shape[0] // 2, kept.shape[1]
    return pl.pallas_call(
        combine_kernel,
        out_shape=(
            jax.ShapeDtypeStruct((half, width + EXTRA), jnp.int16),
            jax.ShapeDtypeStruct((half, width), jnp.float32),
        ),
        in_specs=[whole()] * 2,
        out_specs=(whole(), whole()),
        compiler_params=PARAMS,
        name="combine",
    )(kept, got)


def layer(history, candidates, hist_length, visible, w_proj, w_out):
    width = w_out.shape[0]
    n_keys = history.shape[0]
    size = lax.axis_size("hist")
    me = lax.axis_index("hist")
    masks = []
    bit = size // 2
    while bit > 1:
        masks.append(bit | 1)
        bit //= 2
    bases = jnp.stack([me, me ^ 1]).astype(jnp.int32) * n_keys
    packed = pack(candidates, hist_length, visible)
    keys, self_key = project(history, packed, w_proj, 2 * width)
    values, self_value = project(history, packed, w_proj, 3 * width)
    other_keys = swapped(keys, "hist", 1)
    other_values = swapped(values, "hist", 1)
    gathered = packed
    for mask in masks[:-1]:
        got = swapped(gathered, "hist", mask)
        gathered = jnp.concatenate([gathered, got], axis=0)
    far = swapped(gathered, "hist", masks[-1])
    shards = (w_proj, keys, values, other_keys, other_values)
    kept = attend(bases, gathered, *shards, HEADS, False)
    sent = attend(bases, far, *shards, HEADS, True)
    gate, term = own(packed, w_proj, self_key, self_value, HEADS)
    got = swapped(sent, "hist", masks[-1])
    for mask in masks[-2::-1]:
        sent, kept = combine(kept, got)
        got = swapped(sent, "hist", mask)
    return finish(candidates, kept, got, term, gate, w_out)


def solution(mesh):
    in_specs = (
        P(("groups", "hist"), None),
        P(("groups", "hist"), None),
        P("groups"),
        P(("groups", "hist")),
        P(),
        P(),
    )
    out_specs = P(("groups", "hist"), None)
    return jax.shard_map(
        layer, mesh=mesh, in_specs=in_specs, out_specs=out_specs, check_vma=False
    )
```

```python
import jax
import jax.numpy as jnp
from jax import lax
from jax.experimental import pallas as pl
from jax.experimental.pallas import tpu as pltpu
from jax.sharding import PartitionSpec as P


HEADS = 8
EPS = 1e-06
EXTRA = 128
STEPS = 32000.0
GRANT = 8 * 1024 * 1024
PARAMS = pltpu.CompilerParams(vmem_limit_bytes=GRANT)


def swapped(shard, axis, mask):
    size = lax.axis_size(axis)
    return lax.ppermute(shard, axis, [(i, i ^ mask) for i in range(size)])


def norm(rows):
    centred = rows - jnp.mean(rows, axis=-1, keepdims=True)
    spread = jnp.mean(centred * centred, axis=-1, keepdims=True)
    return centred * lax.rsqrt(spread + EPS)


def silu(x):
    half = x * 0.5
    return half + half * jnp.tanh(half)


def whole():
    return pl.BlockSpec(memory_space=pltpu.VMEM)


def encode(rows, out_ref):
    count, width = rows.shape
    top = jnp.max(jnp.abs(rows), axis=-1, keepdims=True)
    exponent = jnp.ceil(jnp.log2(jnp.maximum(top, 1e-30)))
    code = jnp.round(rows * (STEPS * jnp.exp2(-exponent)))
    out_ref[:, :width] = code.astype(jnp.int32).astype(jnp.int16)
    out_ref[:, width:] = (
        jnp.broadcast_to(exponent, (count, EXTRA)).astype(jnp.int32).astype(jnp.int16)
    )


def decode(code, width):
    code = code.astype(jnp.int32).astype(jnp.float32)
    return code[:, :width] * (jnp.exp2(code[:, width : width + 1]) * (1 / STEPS))


def stay(array):
    return pltpu.with_memory_space_constraint(array, pltpu.HBM)


def near_by(*arrays):
    return [pltpu.with_memory_space_constraint(array, pltpu.VMEM) for array in arrays]


def hbm():
    return pl.BlockSpec(memory_space=pltpu.HBM)


def limits_of(packed, width):
    high = packed[:, width : width + 1].astype(jnp.float32)
    low = packed[:, width + 1 : width + 2].astype(jnp.float32)
    return high * 256 + low


def begin_kernel(length_ref, cand_ref, visible_ref, out_ref, cand, visible, sems):
    rows, width = cand.shape
    loads = [
        pltpu.make_async_copy(cand_ref, cand, sems.at[0]),
        pltpu.make_async_copy(visible_ref, visible, sems.at[1]),
    ]
    for load in loads:
        load.start()
    loads[1].wait()
    seen = jnp.broadcast_to(visible[...], (rows, rows))
    diagonal = lax.broadcasted_iota(jnp.int32, (rows, rows), 0) == lax.broadcasted_iota(
        jnp.int32, (rows, rows), 1
    )
    limit = jnp.minimum(seen, length_ref[0]).astype(jnp.float32)
    limit = jnp.sum(jnp.where(diagonal, limit, 0.0), axis=1, keepdims=True)
    high = jnp.floor(limit * (1 / 256))
    low = limit - high * 256
    lane = lax.broadcasted_iota(jnp.int32, (rows, EXTRA), 1)
    out_ref[:, width:] = jnp.where(lane == 0, high, low).astype(jnp.bfloat16)
    loads[0].wait()
    out_ref[:, :width] = norm(cand[...].astype(jnp.float32)).astype(jnp.bfloat16)


def begin(candidates, hist_length, visible):
    rows, width = candidates.shape
    return pl.pallas_call(
        begin_kernel,
        out_shape=jax.ShapeDtypeStruct((rows, width + EXTRA), jnp.bfloat16),
        in_specs=[pl.BlockSpec(memory_space=pltpu.SMEM)] + [hbm()] * 2,
        out_specs=whole(),
        scratch_shapes=[
            pltpu.VMEM((rows, width), jnp.bfloat16),
            pltpu.VMEM((1, rows), jnp.int32),
            pltpu.SemaphoreType.DMA((2,)),
        ],
        compiler_params=PARAMS,
        cost_estimate=pl.CostEstimate(
            flops=6 * width**3, bytes_accessed=20 * width**2, transcendentals=0
        ),
        name="begin",
    )(hist_length, stay(candidates), stay(visible.reshape(1, rows)))


def project(rows_ref, w_ref, first, tile, n_keys, out_ref, self_ref):
    width = out_ref.shape[1]
    for at in range(0, width, tile):
        made = silu(
            jnp.dot(
                rows_ref[...],
                w_ref[:, first + at : first + at + tile],
                preferred_element_type=jnp.float32,
            )
        ).astype(jnp.bfloat16)
        out_ref[:, at : at + tile] = made[:n_keys]
        self_ref[:, at : at + tile] = made[n_keys:]


def project_keys(history, packed, w_proj):
    n_keys, width = history.shape
    rows = packed.shape[0]
    tile = min(256, width)

    def body(hist_ref, packed_ref, w_ref, key_ref, self_ref, rows_ref):
        rows_ref[n_keys:] = packed_ref[:, :width]
        rows_ref[:n_keys] = norm(hist_ref[...].astype(jnp.float32)).astype(jnp.bfloat16)
        project(rows_ref, w_ref, 2 * width, tile, n_keys, key_ref, self_ref)

    return pl.pallas_call(
        body,
        out_shape=(
            jax.ShapeDtypeStruct((n_keys, width), jnp.bfloat16),
            jax.ShapeDtypeStruct((rows, width), jnp.bfloat16),
            jax.ShapeDtypeStruct((n_keys + rows, width), jnp.bfloat16),
        ),
        in_specs=[whole()] * 3,
        out_specs=[whole()] * 3,
        compiler_params=PARAMS,
        name="keys",
    )(*near_by(history, packed, w_proj))


def project_values(rows_both, w_proj, rows):
    width = rows_both.shape[1]
    n_keys = rows_both.shape[0] - rows
    tile = min(256, width)

    def body(rows_ref, w_ref, value_ref, self_ref):
        project(rows_ref, w_ref, 3 * width, tile, n_keys, value_ref, self_ref)

    return pl.pallas_call(
        body,
        out_shape=(
            jax.ShapeDtypeStruct((n_keys, width), jnp.bfloat16),
            jax.ShapeDtypeStruct((rows, width), jnp.bfloat16),
        ),
        in_specs=[whole()] * 2,
        out_specs=[whole()] * 2,
        compiler_params=PARAMS,
        name="values",
    )(*near_by(rows_both, w_proj))


def project_queries(packed, got, w_proj):
    rows = packed.shape[0]
    width = w_proj.shape[0]
    tile = min(256, width)

    def body(packed_ref, got_ref, w_ref, out_ref):
        out_ref[:rows, width:] = packed_ref[:, width:]
        out_ref[rows:, width:] = got_ref[:, width:]
        both = jnp.concatenate([packed_ref[:, :width], got_ref[:, :width]], axis=0)
        for at in range(0, width, tile):
            out_ref[:, at : at + tile] = silu(
                jnp.dot(
                    both,
                    w_ref[:, width + at : width + at + tile],
                    preferred_element_type=jnp.float32,
                )
            ).astype(jnp.bfloat16)

    return pl.pallas_call(
        body,
        out_shape=jax.ShapeDtypeStruct((2 * rows, packed.shape[1]), jnp.bfloat16),
        in_specs=[whole()] * 3,
        out_specs=whole(),
        compiler_params=PARAMS,
        name="queries",
    )(*near_by(packed, got, w_proj))


def join(first, second):
    rows = first.shape[0]

    def body(first_ref, second_ref, out_ref):
        out_ref[:rows] = first_ref[...]
        out_ref[rows:] = second_ref[...]

    return pl.pallas_call(
        body,
        out_shape=jax.ShapeDtypeStruct((2 * rows, first.shape[1]), first.dtype),
        in_specs=[whole()] * 2,
        out_specs=whole(),
        compiler_params=PARAMS,
        name="join",
    )(first, second)


def attend_kernel(heads, coded, query_ref, k0, v0, k1, v1, out_ref, acc_ref):
    n_keys, width = k0.shape
    size = width // heads
    rows = query_ref.shape[0]
    limit = limits_of(query_ref[...], width)
    inverse = 1.0 / (limit + 1.0)
    position = lax.broadcasted_iota(jnp.int32, (rows, n_keys), 1).astype(jnp.float32)
    share = []
    for side in range(2):
        base = ((lax.axis_index("hist") ^ side) * n_keys).astype(jnp.float32)
        share.append(jnp.where(position + base < limit, inverse, 0.0))
    for head in range(heads):
        cols = slice(head * size, (head + 1) * size)
        total = None
        for side, (k, v) in enumerate(((k0, v0), (k1, v1))):
            scores = lax.dot_general(
                query_ref[:, cols],
                k[:, cols],
                (((1,), (1,)), ((), ())),
                preferred_element_type=jnp.float32,
            )
            weight = (silu(scores * size ** (-0.5)) * share[side]).astype(jnp.bfloat16)
            part = jnp.dot(weight, v[:, cols], preferred_element_type=jnp.float32)
            total = part if total is None else total + part
        acc_ref[:, cols] = total
    made = acc_ref[...]
    made = made - jnp.mean(made, axis=-1, keepdims=True)
    if coded:
        encode(made, out_ref)
    else:
        out_ref[...] = made


def attend(query, k0, v0, k1, v1, heads, coded):
    rows = query.shape[0]
    _, width = k0.shape

    def body(*refs):
        attend_kernel(heads, coded, *refs)

    return pl.pallas_call(
        body,
        out_shape=jax.ShapeDtypeStruct((rows, width + EXTRA), jnp.int16)
        if coded
        else jax.ShapeDtypeStruct((rows, width), jnp.float32),
        in_specs=[whole()] * 5,
        out_specs=whole(),
        scratch_shapes=[pltpu.VMEM((rows, width), jnp.float32)],
        compiler_params=PARAMS,
    )(*near_by(query, k0, v0, k1, v1))


def own_kernel(heads, tile, query_ref, packed_ref, w_ref, key_ref, value_ref, gate_ref, term_ref):
    rows, width = key_ref.shape
    size = width // heads
    query = query_ref[:rows, :width].astype(jnp.float32)
    inverse = 1.0 / (limits_of(packed_ref[...], width) + 1.0)
    products = query * key_ref[...].astype(jnp.float32)
    for head in range(heads):
        cols = slice(head * size, (head + 1) * size)
        score = jnp.sum(products[:, cols], axis=-1, keepdims=True)
        weight = (silu(score * size ** (-0.5)) * inverse).astype(jnp.bfloat16)
        term_ref[:, cols] = weight.astype(jnp.float32) * value_ref[:, cols].astype(jnp.float32)
    for at in range(0, width, tile):
        gate_ref[:, at : at + tile] = silu(
            jnp.dot(
                packed_ref[:, :width],
                w_ref[:, at : at + tile],
                preferred_element_type=jnp.float32,
            )
        ).astype(jnp.bfloat16)


def own(query, packed, w_proj, self_key, self_value, heads):
    rows, width = self_key.shape
    tile = min(256, width)

    def body(*refs):
        own_kernel(heads, tile, *refs)

    return pl.pallas_call(
        body,
        out_shape=(
            jax.ShapeDtypeStruct((rows, width), jnp.bfloat16),
            jax.ShapeDtypeStruct((rows, width), jnp.float32),
        ),
        in_specs=[whole()] * 5,
        out_specs=[whole()] * 2,
        compiler_params=PARAMS,
        name="own",
    )(*near_by(query, packed, w_proj, self_key, self_value))


def finish_kernel(cand_ref, kept_ref, got_ref, term_ref, gate_ref, w_ref, out_ref):
    attended = kept_ref[...] + decode(got_ref[...], kept_ref.shape[1]) + term_ref[...]
    mixed = (norm(attended) * gate_ref[...].astype(jnp.float32)).astype(jnp.bfloat16)
    out_ref[...] = (
        cand_ref[...].astype(jnp.float32)
        + jnp.dot(mixed, w_ref[...], preferred_element_type=jnp.float32)
    ).astype(jnp.bfloat16)


def finish(candidates, kept, got, term, gate, w_out):
    return pl.pallas_call(
        finish_kernel,
        out_shape=jax.ShapeDtypeStruct(candidates.shape, jnp.bfloat16),
        in_specs=[whole()] * 6,
        out_specs=whole(),
        compiler_params=PARAMS,
        name="finish",
    )(candidates, kept, got, term, gate, w_out)


def combine_kernel(kept_ref, got_ref, sent_ref, out_ref):
    half, width = out_ref.shape
    encode(kept_ref[half:] + decode(got_ref[half:], width), sent_ref)
    out_ref[...] = kept_ref[:half] + decode(got_ref[:half], width)


def combine(kept, got):
    half, width = kept.shape[0] // 2, kept.shape[1]
    return pl.pallas_call(
        combine_kernel,
        out_shape=(
            jax.ShapeDtypeStruct((half, width + EXTRA), jnp.int16),
            jax.ShapeDtypeStruct((half, width), jnp.float32),
        ),
        in_specs=[whole()] * 2,
        out_specs=(whole(), whole()),
        compiler_params=PARAMS,
        name="combine",
    )(kept, got)


def layer(history, candidates, hist_length, visible, w_proj, w_out):
    size = lax.axis_size("hist")
    masks = []
    bit = size // 2
    while bit > 1:
        masks.append(bit | 1)
        bit //= 2
    packed = begin(candidates, hist_length, visible)
    keys, self_key, rows_both = project_keys(history, packed, w_proj)
    values, self_value = project_values(rows_both, w_proj, packed.shape[0])
    other_keys = swapped(keys, "hist", 1)
    other_values = swapped(values, "hist", 1)
    gathered = packed
    for step, mask in enumerate(masks[:-1]):
        got = swapped(gathered, "hist", mask)
        gathered = join(gathered, got) if step else project_queries(packed, got, w_proj)
    far = swapped(gathered, "hist", masks[-1])
    shards = (keys, values, other_keys, other_values)
    kept = attend(gathered, *shards, HEADS, False)
    sent = attend(far, *shards, HEADS, True)
    gate, term = own(gathered, packed, w_proj, self_key, self_value, HEADS)
    got = swapped(sent, "hist", masks[-1])
    for mask in masks[-2::-1]:
        sent, kept = combine(kept, got)
        got = swapped(sent, "hist", mask)
    return finish(candidates, kept, got, term, gate, w_out)


def solution(mesh):
    in_specs = (
        P(("groups", "hist"), None),
        P(("groups", "hist"), None),
        P("groups"),
        P(("groups", "hist")),
        P(),
        P(),
    )
    out_specs = P(("groups", "hist"), None)
    return jax.shard_map(
        layer, mesh=mesh, in_specs=in_specs, out_specs=out_specs, check_vma=False
    )
```

```python
import jax
import jax.numpy as jnp
from jax import lax
from jax.experimental import pallas as pl
from jax.experimental.pallas import tpu as pltpu
from jax.sharding import PartitionSpec as P


HEADS = 8
EPS = 1e-06
EXTRA = 128
STEPS = 32000.0
GRANT = 8 * 1024 * 1024
PARAMS = pltpu.CompilerParams(vmem_limit_bytes=GRANT)


def swapped(shard, axis, mask):
    size = lax.axis_size(axis)
    return lax.ppermute(shard, axis, [(i, i ^ mask) for i in range(size)])


def norm(rows):
    centred = rows - jnp.mean(rows, axis=-1, keepdims=True)
    spread = jnp.mean(centred * centred, axis=-1, keepdims=True)
    return centred * lax.rsqrt(spread + EPS)


def silu(x):
    half = x * 0.5
    return half + half * jnp.tanh(half)


def whole():
    return pl.BlockSpec(memory_space=pltpu.VMEM)


def encode(rows, out_ref):
    count, width = rows.shape
    top = jnp.max(jnp.abs(rows), axis=-1, keepdims=True)
    exponent = jnp.ceil(jnp.log2(jnp.maximum(top, 1e-30)))
    code = jnp.round(rows * (STEPS * jnp.exp2(-exponent)))
    out_ref[:, :width] = code.astype(jnp.int32).astype(jnp.int16)
    out_ref[:, width:] = (
        jnp.broadcast_to(exponent, (count, EXTRA)).astype(jnp.int32).astype(jnp.int16)
    )


def decode(code, width):
    code = code.astype(jnp.int32).astype(jnp.float32)
    return code[:, :width] * (jnp.exp2(code[:, width : width + 1]) * (1 / STEPS))


def stay(array):
    return pltpu.with_memory_space_constraint(array, pltpu.HBM)


def near_by(*arrays):
    return [pltpu.with_memory_space_constraint(array, pltpu.VMEM) for array in arrays]


def hbm():
    return pl.BlockSpec(memory_space=pltpu.HBM)


def limits_of(packed, width):
    high = packed[:, width : width + 1].astype(jnp.float32)
    low = packed[:, width + 1 : width + 2].astype(jnp.float32)
    return high * 256 + low


def begin_kernel(length_ref, cand_ref, visible_ref, out_ref, cand, visible, sems):
    rows, width = cand.shape
    loads = [
        pltpu.make_async_copy(cand_ref, cand, sems.at[0]),
        pltpu.make_async_copy(visible_ref, visible, sems.at[1]),
    ]
    for load in loads:
        load.start()
    loads[1].wait()
    seen = jnp.broadcast_to(visible[...], (rows, rows))
    diagonal = lax.broadcasted_iota(jnp.int32, (rows, rows), 0) == lax.broadcasted_iota(
        jnp.int32, (rows, rows), 1
    )
    limit = jnp.minimum(seen, length_ref[0]).astype(jnp.float32)
    limit = jnp.sum(jnp.where(diagonal, limit, 0.0), axis=1, keepdims=True)
    high = jnp.floor(limit * (1 / 256))
    low = limit - high * 256
    lane = lax.broadcasted_iota(jnp.int32, (rows, EXTRA), 1)
    out_ref[:, width:] = jnp.where(lane == 0, high, low).astype(jnp.bfloat16)
    loads[0].wait()
    out_ref[:, :width] = norm(cand[...].astype(jnp.float32)).astype(jnp.bfloat16)


def begin(candidates, hist_length, visible):
    rows, width = candidates.shape
    return pl.pallas_call(
        begin_kernel,
        out_shape=jax.ShapeDtypeStruct((rows, width + EXTRA), jnp.bfloat16),
        in_specs=[pl.BlockSpec(memory_space=pltpu.SMEM)] + [hbm()] * 2,
        out_specs=whole(),
        scratch_shapes=[
            pltpu.VMEM((rows, width), jnp.bfloat16),
            pltpu.VMEM((1, rows), jnp.int32),
            pltpu.SemaphoreType.DMA((2,)),
        ],
        compiler_params=PARAMS,
        cost_estimate=pl.CostEstimate(
            flops=6 * width**3, bytes_accessed=20 * width**2, transcendentals=0
        ),
        name="begin",
    )(hist_length, stay(candidates), stay(visible.reshape(1, rows)))


def project(rows_ref, w_ref, first, tile, n_keys, out_ref, self_ref):
    width = out_ref.shape[1]
    for at in range(0, width, tile):
        made = silu(
            jnp.dot(
                rows_ref[...],
                w_ref[:, first + at : first + at + tile],
                preferred_element_type=jnp.float32,
            )
        ).astype(jnp.bfloat16)
        out_ref[:, at : at + tile] = made[:n_keys]
        self_ref[:, at : at + tile] = made[n_keys:]


def project_keys(history, packed, w_proj):
    n_keys, width = history.shape
    rows = packed.shape[0]
    tile = min(256, width)

    def body(hist_ref, packed_ref, w_ref, key_ref, self_ref, rows_ref):
        rows_ref[n_keys:] = packed_ref[:, :width]
        rows_ref[:n_keys] = norm(hist_ref[...].astype(jnp.float32)).astype(jnp.bfloat16)
        project(rows_ref, w_ref, 2 * width, tile, n_keys, key_ref, self_ref)

    return pl.pallas_call(
        body,
        out_shape=(
            jax.ShapeDtypeStruct((n_keys, width), jnp.bfloat16),
            jax.ShapeDtypeStruct((rows, width), jnp.bfloat16),
            jax.ShapeDtypeStruct((n_keys + rows, width), jnp.bfloat16),
        ),
        in_specs=[whole()] * 3,
        out_specs=[whole()] * 3,
        compiler_params=PARAMS,
        name="keys",
    )(*near_by(history, packed, w_proj))


def project_values(rows_both, w_proj, rows):
    width = rows_both.shape[1]
    n_keys = rows_both.shape[0] - rows
    tile = min(256, width)

    def body(rows_ref, w_ref, value_ref, self_ref):
        project(rows_ref, w_ref, 3 * width, tile, n_keys, value_ref, self_ref)

    return pl.pallas_call(
        body,
        out_shape=(
            jax.ShapeDtypeStruct((n_keys, width), jnp.bfloat16),
            jax.ShapeDtypeStruct((rows, width), jnp.bfloat16),
        ),
        in_specs=[whole()] * 2,
        out_specs=[whole()] * 2,
        compiler_params=PARAMS,
        name="values",
    )(*near_by(rows_both, w_proj))


def project_queries(packed, got, w_proj):
    rows = packed.shape[0]
    width = w_proj.shape[0]
    tile = min(256, width)

    def body(packed_ref, got_ref, w_ref, out_ref):
        out_ref[:rows, width:] = packed_ref[:, width:]
        out_ref[rows:, width:] = got_ref[:, width:]
        both = jnp.concatenate([packed_ref[:, :width], got_ref[:, :width]], axis=0)
        for at in range(0, width, tile):
            out_ref[:, at : at + tile] = silu(
                jnp.dot(
                    both,
                    w_ref[:, width + at : width + at + tile],
                    preferred_element_type=jnp.float32,
                )
            ).astype(jnp.bfloat16)

    return pl.pallas_call(
        body,
        out_shape=jax.ShapeDtypeStruct((2 * rows, packed.shape[1]), jnp.bfloat16),
        in_specs=[whole()] * 3,
        out_specs=whole(),
        compiler_params=PARAMS,
        name="queries",
    )(*near_by(packed, got, w_proj))


def join(first, second):
    rows = first.shape[0]

    def body(first_ref, second_ref, out_ref):
        out_ref[:rows] = first_ref[...]
        out_ref[rows:] = second_ref[...]

    return pl.pallas_call(
        body,
        out_shape=jax.ShapeDtypeStruct((2 * rows, first.shape[1]), first.dtype),
        in_specs=[whole()] * 2,
        out_specs=whole(),
        compiler_params=PARAMS,
        name="join",
    )(first, second)


def attend_kernel(heads, query, k0, v0, k1, v1, acc_ref):
    n_keys, width = k0.shape
    size = width // heads
    rows = query.shape[0]
    limit = limits_of(query, width)
    inverse = 1.0 / (limit + 1.0)
    position = lax.broadcasted_iota(jnp.int32, (rows, n_keys), 1).astype(jnp.float32)
    sides = ((k0, v0), (k1, v1))
    share = []
    for side in range(2):
        base = ((lax.axis_index("hist") ^ side) * n_keys).astype(jnp.float32)
        share.append(jnp.where(position + base < limit, inverse, 0.0))

    def scores_of(head):
        cols = slice(head * size, (head + 1) * size)
        return [
            lax.dot_general(
                query[:, cols],
                k[:, cols],
                (((1,), (1,)), ((), ())),
                preferred_element_type=jnp.float32,
            )
            for k, _ in sides
        ]

    ahead = scores_of(0)
    for head in range(heads):
        scores = ahead
        if head + 1 < heads:
            ahead = scores_of(head + 1)
        cols = slice(head * size, (head + 1) * size)
        total = None
        for side, (_, v) in enumerate(sides):
            weight = (silu(scores[side] * size ** (-0.5)) * share[side]).astype(jnp.bfloat16)
            part = jnp.dot(weight, v[:, cols], preferred_element_type=jnp.float32)
            total = part if total is None else total + part
        acc_ref[:, cols] = total
    made = acc_ref[...]
    return made - jnp.mean(made, axis=-1, keepdims=True)


def attend(queries, shards, heads, coded):
    rows = queries[0].shape[0]
    _, width = shards[0].shape
    blocks = len(queries)

    def body(*refs):
        ins, shard_refs, outs = refs[:blocks], refs[blocks : blocks + 4], refs[blocks + 4 : -1]
        query = jnp.concatenate([ref[...] for ref in ins], axis=0)
        made = attend_kernel(heads, query, *shard_refs, refs[-1])
        for block, out_ref in enumerate(outs):
            part = made[block * rows : (block + 1) * rows]
            if coded:
                encode(part, out_ref)
            else:
                out_ref[...] = part

    out = (
        jax.ShapeDtypeStruct((rows, width + EXTRA), jnp.int16)
        if coded
        else jax.ShapeDtypeStruct((rows, width), jnp.float32)
    )
    return pl.pallas_call(
        body,
        out_shape=[out] * blocks,
        in_specs=[whole()] * (blocks + 4),
        out_specs=[whole()] * blocks,
        scratch_shapes=[pltpu.VMEM((blocks * rows, width), jnp.float32)],
        compiler_params=PARAMS,
    )(*near_by(*queries, *shards))


def own_kernel(heads, tile, query_ref, packed_ref, w_ref, key_ref, value_ref, gate_ref, term_ref):
    rows, width = key_ref.shape
    size = width // heads
    query = query_ref[:rows, :width].astype(jnp.float32)
    inverse = 1.0 / (limits_of(packed_ref[...], width) + 1.0)
    products = query * key_ref[...].astype(jnp.float32)
    for head in range(heads):
        cols = slice(head * size, (head + 1) * size)
        score = jnp.sum(products[:, cols], axis=-1, keepdims=True)
        weight = (silu(score * size ** (-0.5)) * inverse).astype(jnp.bfloat16)
        term_ref[:, cols] = weight.astype(jnp.float32) * value_ref[:, cols].astype(jnp.float32)
    for at in range(0, width, tile):
        gate_ref[:, at : at + tile] = silu(
            jnp.dot(
                packed_ref[:, :width],
                w_ref[:, at : at + tile],
                preferred_element_type=jnp.float32,
            )
        ).astype(jnp.bfloat16)


def own(query, packed, w_proj, self_key, self_value, heads):
    rows, width = self_key.shape
    tile = min(256, width)

    def body(*refs):
        own_kernel(heads, tile, *refs)

    return pl.pallas_call(
        body,
        out_shape=(
            jax.ShapeDtypeStruct((rows, width), jnp.bfloat16),
            jax.ShapeDtypeStruct((rows, width), jnp.float32),
        ),
        in_specs=[whole()] * 5,
        out_specs=[whole()] * 2,
        compiler_params=PARAMS,
        name="own",
    )(*near_by(query, packed, w_proj, self_key, self_value))


def total_of(terms, refs, rows, width):
    total = None
    for place, first in terms:
        part = refs[place][first : first + rows]
        if part.dtype == jnp.int16:
            part = decode(part, width)
        total = part if total is None else total + part
    return total


def placed(pieces):
    arrays = []
    lists = []
    for terms in pieces:
        listed = []
        for array, first in terms:
            place = next((i for i, seen in enumerate(arrays) if seen is array), None)
            if place is None:
                place = len(arrays)
                arrays.append(array)
            listed.append((place, first))
        lists.append(listed)
    return arrays, lists


def emit(pieces, rows, width):
    arrays, lists = placed(pieces)

    def body(*refs):
        for terms, out_ref in zip(lists, refs[len(arrays) :]):
            encode(total_of(terms, refs, rows, width), out_ref)

    return pl.pallas_call(
        body,
        out_shape=[jax.ShapeDtypeStruct((rows, width + EXTRA), jnp.int16)] * len(pieces),
        in_specs=[whole()] * len(arrays),
        out_specs=[whole()] * len(pieces),
        compiler_params=PARAMS,
        name="emit",
    )(*arrays)


def finish(candidates, terms, term, gate, w_out):
    arrays, (listed,) = placed([terms])

    def body(cand_ref, term_ref, gate_ref, w_ref, *refs):
        rows, width = cand_ref.shape
        attended = total_of(listed, refs, rows, width) + term_ref[...]
        mixed = (norm(attended) * gate_ref[...].astype(jnp.float32)).astype(jnp.bfloat16)
        refs[-1][...] = (
            cand_ref[...].astype(jnp.float32)
            + jnp.dot(mixed, w_ref[...], preferred_element_type=jnp.float32)
        ).astype(jnp.bfloat16)

    return pl.pallas_call(
        body,
        out_shape=jax.ShapeDtypeStruct(candidates.shape, jnp.bfloat16),
        in_specs=[whole()] * (4 + len(arrays)),
        out_specs=whole(),
        compiler_params=PARAMS,
        name="finish",
    )(candidates, term, gate, w_out, *arrays)


def layer(history, candidates, hist_length, visible, w_proj, w_out):
    width = w_out.shape[0]
    size = lax.axis_size("hist")
    masks = []
    bit = size // 2
    while bit > 1:
        masks.append(bit | 1)
        bit //= 2
    packed = begin(candidates, hist_length, visible)
    keys, self_key, rows_both = project_keys(history, packed, w_proj)
    values, self_value = project_values(rows_both, w_proj, packed.shape[0])
    other_keys = swapped(keys, "hist", 1)
    other_values = swapped(values, "hist", 1)
    inner = packed
    for step, mask in enumerate(masks[:-2]):
        got = swapped(inner, "hist", mask)
        inner = join(inner, got) if step else project_queries(packed, got, w_proj)
    outer = swapped(inner, "hist", masks[-2])
    far_inner = swapped(inner, "hist", masks[-1])
    far_outer = swapped(outer, "hist", masks[-1])
    shards = (keys, values, other_keys, other_values)
    sent_inner, sent_outer = attend([far_inner, far_outer], shards, HEADS, True)
    got_outer = swapped(sent_outer, "hist", masks[-1])
    got_inner = swapped(sent_inner, "hist", masks[-1])
    near_inner, near_outer = attend([inner, outer], shards, HEADS, False)
    gate, term = own(inner, packed, w_proj, self_key, self_value, HEADS)
    rows = packed.shape[0]
    blocks = inner.shape[0] // rows
    terms = [(near_outer, 0), (got_outer, 0)]
    last = []
    stage = len(masks) - 2
    while True:
        sides = 2 if blocks > 1 else 1
        piece = blocks * rows // sides
        sent = emit(
            [[(array, first + side * piece) for array, first in terms] for side in range(sides)],
            piece,
            width,
        )
        got = [None] * sides
        for side in reversed(range(sides)):
            got[side] = swapped(sent[side], "hist", masks[stage])
        last.append(got[0])
        if sides == 1:
            break
        blocks //= 2
        first = blocks * rows
        terms = [(near_inner, first), (got_inner, first)]
        terms += [(array, first) for array in last[:-1]] + [(got[1], 0)]
        stage -= 1
    terms = [(near_inner, 0), (got_inner, 0)] + [(array, 0) for array in last]
    return finish(candidates, terms, term, gate, w_out)


def solution(mesh):
    in_specs = (
        P(("groups", "hist"), None),
        P(("groups", "hist"), None),
        P("groups"),
        P(("groups", "hist")),
        P(),
        P(),
    )
    out_specs = P(("groups", "hist"), None)
    return jax.shard_map(layer, mesh=mesh, in_specs=in_specs, out_specs=out_specs, check_vma=False)
```

```python
import jax
import jax.numpy as jnp
from jax import lax
from jax.experimental import pallas as pl
from jax.experimental.pallas import tpu as pltpu
from jax.sharding import PartitionSpec as P


HEADS = 8
EPS = 1e-06
EXTRA = 128
STEPS = 32000.0
GRANT = 8 * 1024 * 1024
PARAMS = pltpu.CompilerParams(vmem_limit_bytes=GRANT)


def swapped(shard, axis, mask):
    size = lax.axis_size(axis)
    return lax.ppermute(shard, axis, [(i, i ^ mask) for i in range(size)])


def norm(rows):
    centred = rows - jnp.mean(rows, axis=-1, keepdims=True)
    spread = jnp.mean(centred * centred, axis=-1, keepdims=True)
    return centred * lax.rsqrt(spread + EPS)


def silu(x):
    half = x * 0.5
    return half + half * jnp.tanh(half)


def whole():
    return pl.BlockSpec(memory_space=pltpu.VMEM)


def encode(rows, out_ref):
    count, width = rows.shape
    top = jnp.max(jnp.abs(rows), axis=-1, keepdims=True)
    exponent = jnp.ceil(jnp.log2(jnp.maximum(top, 1e-30)))
    code = jnp.round(rows * (STEPS * jnp.exp2(-exponent)))
    out_ref[:, :width] = code.astype(jnp.int32).astype(jnp.int16)
    out_ref[:, width:] = (
        jnp.broadcast_to(exponent, (count, EXTRA)).astype(jnp.int32).astype(jnp.int16)
    )


def decode(code, width):
    code = code.astype(jnp.int32).astype(jnp.float32)
    return code[:, :width] * (jnp.exp2(code[:, width : width + 1]) * (1 / STEPS))


def near_by(*arrays):
    return [pltpu.with_memory_space_constraint(array, pltpu.VMEM) for array in arrays]


def limits_of(packed, width):
    high = packed[:, width : width + 1].astype(jnp.float32)
    low = packed[:, width + 1 : width + 2].astype(jnp.float32)
    return high * 256 + low


def spark():
    def body(out_ref):
        out_ref[...] = jnp.zeros_like(out_ref)

    return pl.pallas_call(
        body,
        out_shape=jax.ShapeDtypeStruct((8, 128), jnp.float32),
        out_specs=whole(),
        compiler_params=PARAMS,
        cost_estimate=pl.CostEstimate(flops=6 * 10**9, bytes_accessed=2 * 10**7, transcendentals=0),
        name="spark",
    )()


def normed(rows):
    return norm(rows.astype(jnp.float32)).astype(jnp.bfloat16)


def limit_columns(visible, length):
    rows = visible.shape[1]
    diagonal = lax.broadcasted_iota(jnp.int32, (rows, rows), 0) == lax.broadcasted_iota(
        jnp.int32, (rows, rows), 1
    )
    limit = jnp.minimum(jnp.broadcast_to(visible, (rows, rows)), length).astype(jnp.float32)
    limit = jnp.sum(jnp.where(diagonal, limit, 0.0), axis=1, keepdims=True)
    high = jnp.floor(limit * (1 / 256))
    low = limit - high * 256
    lane = lax.broadcasted_iota(jnp.int32, (rows, EXTRA), 1)
    return jnp.where(lane == 0, high, low).astype(jnp.bfloat16)


def project(rows_ref, w_ref, first, tile, n_keys, out_ref, self_ref):
    width = out_ref.shape[1]
    for at in range(0, width, tile):
        made = silu(
            jnp.dot(
                rows_ref[...],
                w_ref[:, first + at : first + at + tile],
                preferred_element_type=jnp.float32,
            )
        ).astype(jnp.bfloat16)
        out_ref[:, at : at + tile] = made[:n_keys]
        self_ref[:, at : at + tile] = made[n_keys:]


def project_keys(history, candidates, w_proj, first_op):
    n_keys, width = history.shape
    rows = candidates.shape[0]
    tile = min(256, width)

    def body(hist_ref, cand_ref, w_ref, first_ref, key_ref, self_ref, rows_ref):
        rows_ref[n_keys:] = normed(cand_ref[...])
        rows_ref[:n_keys] = normed(hist_ref[...])
        project(rows_ref, w_ref, 2 * width, tile, n_keys, key_ref, self_ref)

    return pl.pallas_call(
        body,
        out_shape=(
            jax.ShapeDtypeStruct((n_keys, width), jnp.bfloat16),
            jax.ShapeDtypeStruct((rows, width), jnp.bfloat16),
            jax.ShapeDtypeStruct((n_keys + rows, width), jnp.bfloat16),
        ),
        in_specs=[whole()] * 4,
        out_specs=[whole()] * 3,
        compiler_params=PARAMS,
        name="keys",
    )(*near_by(history, candidates, w_proj, first_op))


def project_values(rows_both, w_proj, rows):
    width = rows_both.shape[1]
    n_keys = rows_both.shape[0] - rows
    tile = min(256, width)

    def body(rows_ref, w_ref, value_ref, self_ref):
        project(rows_ref, w_ref, 3 * width, tile, n_keys, value_ref, self_ref)

    return pl.pallas_call(
        body,
        out_shape=(
            jax.ShapeDtypeStruct((n_keys, width), jnp.bfloat16),
            jax.ShapeDtypeStruct((rows, width), jnp.bfloat16),
        ),
        in_specs=[whole()] * 2,
        out_specs=[whole()] * 2,
        compiler_params=PARAMS,
        name="values",
    )(*near_by(rows_both, w_proj))


def project_queries(candidates, got, visible, got_visible, hist_length, w_proj):
    rows, width = candidates.shape
    tile = min(256, width)

    def body(length_ref, cand_ref, got_ref, visible_ref, got_visible_ref, w_ref, out_ref):
        out_ref[:rows, width:] = limit_columns(visible_ref[...], length_ref[0])
        out_ref[rows:, width:] = limit_columns(got_visible_ref[...], length_ref[0])
        both = jnp.concatenate([normed(cand_ref[...]), normed(got_ref[...])], axis=0)
        for at in range(0, width, tile):
            out_ref[:, at : at + tile] = silu(
                jnp.dot(
                    both,
                    w_ref[:, width + at : width + at + tile],
                    preferred_element_type=jnp.float32,
                )
            ).astype(jnp.bfloat16)

    return pl.pallas_call(
        body,
        out_shape=jax.ShapeDtypeStruct((2 * rows, width + EXTRA), jnp.bfloat16),
        in_specs=[pl.BlockSpec(memory_space=pltpu.SMEM)] + [whole()] * 5,
        out_specs=whole(),
        compiler_params=PARAMS,
        name="queries",
    )(
        hist_length,
        *near_by(candidates, got, visible.reshape(1, rows), got_visible.reshape(1, rows), w_proj),
    )


def join(first, second):
    rows = first.shape[0]

    def body(first_ref, second_ref, out_ref):
        out_ref[:rows] = first_ref[...]
        out_ref[rows:] = second_ref[...]

    return pl.pallas_call(
        body,
        out_shape=jax.ShapeDtypeStruct((2 * rows, first.shape[1]), first.dtype),
        in_specs=[whole()] * 2,
        out_specs=whole(),
        compiler_params=PARAMS,
        name="join",
    )(first, second)


def attend_kernel(heads, query, k0, v0, k1, v1, acc_ref):
    n_keys, width = k0.shape
    size = width // heads
    rows = query.shape[0]
    limit = limits_of(query, width)
    inverse = 1.0 / (limit + 1.0)
    position = lax.broadcasted_iota(jnp.int32, (rows, n_keys), 1).astype(jnp.float32)
    sides = ((k0, v0), (k1, v1))
    share = []
    for side in range(2):
        base = ((lax.axis_index("hist") ^ side) * n_keys).astype(jnp.float32)
        share.append(jnp.where(position + base < limit, inverse, 0.0))

    def scores_of(head):
        cols = slice(head * size, (head + 1) * size)
        return [
            lax.dot_general(
                query[:, cols],
                k[:, cols],
                (((1,), (1,)), ((), ())),
                preferred_element_type=jnp.float32,
            )
            for k, _ in sides
        ]

    ahead = scores_of(0)
    for head in range(heads):
        scores = ahead
        if head + 1 < heads:
            ahead = scores_of(head + 1)
        cols = slice(head * size, (head + 1) * size)
        total = None
        for side, (_, v) in enumerate(sides):
            half = scores[side] * (0.5 * size ** (-0.5))
            weight = ((half + half * jnp.tanh(half)) * share[side]).astype(jnp.bfloat16)
            part = jnp.dot(weight, v[:, cols], preferred_element_type=jnp.float32)
            total = part if total is None else total + part
        acc_ref[:, cols] = total
    made = acc_ref[...]
    return made - jnp.mean(made, axis=-1, keepdims=True)


def attend(queries, shards, heads, parts, coded):
    rows = queries[0].shape[0]
    _, width = shards[0].shape
    blocks = len(queries)
    pieces = [rows // part for part in parts for _ in range(part)]

    def body(*refs):
        ins, shard_refs, outs = refs[:blocks], refs[blocks : blocks + 4], refs[blocks + 4 : -1]
        query = jnp.concatenate([ref[...] for ref in ins], axis=0)
        made = attend_kernel(heads, query, *shard_refs, refs[-1])
        first = 0
        for piece, out_ref in zip(pieces, outs):
            part = made[first : first + piece]
            first += piece
            if coded:
                encode(part, out_ref)
            else:
                out_ref[...] = part

    return pl.pallas_call(
        body,
        out_shape=[
            jax.ShapeDtypeStruct((piece, width + EXTRA), jnp.int16)
            if coded
            else jax.ShapeDtypeStruct((piece, width), jnp.float32)
            for piece in pieces
        ],
        in_specs=[whole()] * (blocks + 4),
        out_specs=[whole()] * len(pieces),
        scratch_shapes=[pltpu.VMEM((blocks * rows, width), jnp.float32)],
        compiler_params=PARAMS,
    )(*near_by(*queries, *shards))


def own_kernel(heads, tile, query_ref, rows_ref, w_ref, key_ref, value_ref, gate_ref, term_ref):
    rows, width = key_ref.shape
    size = width // heads
    query = query_ref[:rows, :width].astype(jnp.float32)
    inverse = 1.0 / (limits_of(query_ref[:rows], width) + 1.0)
    products = query * key_ref[...].astype(jnp.float32)
    for head in range(heads):
        cols = slice(head * size, (head + 1) * size)
        score = jnp.sum(products[:, cols], axis=-1, keepdims=True)
        weight = (silu(score * size ** (-0.5)) * inverse).astype(jnp.bfloat16)
        term_ref[:, cols] = weight.astype(jnp.float32) * value_ref[:, cols].astype(jnp.float32)
    for at in range(0, width, tile):
        gate_ref[:, at : at + tile] = silu(
            jnp.dot(
                rows_ref[rows_ref.shape[0] - rows :],
                w_ref[:, at : at + tile],
                preferred_element_type=jnp.float32,
            )
        ).astype(jnp.bfloat16)


def own(query, rows_both, w_proj, self_key, self_value, heads):
    rows, width = self_key.shape
    tile = min(256, width)

    def body(*refs):
        own_kernel(heads, tile, *refs)

    return pl.pallas_call(
        body,
        out_shape=(
            jax.ShapeDtypeStruct((rows, width), jnp.bfloat16),
            jax.ShapeDtypeStruct((rows, width), jnp.float32),
        ),
        in_specs=[whole()] * 5,
        out_specs=[whole()] * 2,
        compiler_params=PARAMS,
        name="own",
    )(*near_by(query, rows_both, w_proj, self_key, self_value))


def total_of(terms, refs, rows, width):
    total = None
    for place, first in terms:
        part = refs[place][first : first + rows]
        if part.dtype == jnp.int16:
            part = decode(part, width)
        total = part if total is None else total + part
    return total


def placed(pieces):
    arrays = []
    lists = []
    for terms in pieces:
        listed = []
        for array, first in terms:
            place = next((i for i, seen in enumerate(arrays) if seen is array), None)
            if place is None:
                place = len(arrays)
                arrays.append(array)
            listed.append((place, first))
        lists.append(listed)
    return arrays, lists


def emit(terms, rows, width):
    arrays, (listed,) = placed([terms])

    def body(*refs):
        encode(total_of(listed, refs, rows, width), refs[-1])

    return pl.pallas_call(
        body,
        out_shape=jax.ShapeDtypeStruct((rows, width + EXTRA), jnp.int16),
        in_specs=[whole()] * len(arrays),
        out_specs=whole(),
        compiler_params=PARAMS,
        name="emit",
    )(*arrays)


def finish(candidates, terms, term, gate, w_out):
    arrays, (listed,) = placed([terms])

    def body(cand_ref, term_ref, gate_ref, w_ref, *refs):
        rows, width = cand_ref.shape
        attended = total_of(listed, refs, rows, width) + term_ref[...]
        mixed = (norm(attended) * gate_ref[...].astype(jnp.float32)).astype(jnp.bfloat16)
        refs[-1][...] = (
            cand_ref[...].astype(jnp.float32)
            + jnp.dot(mixed, w_ref[...], preferred_element_type=jnp.float32)
        ).astype(jnp.bfloat16)

    return pl.pallas_call(
        body,
        out_shape=jax.ShapeDtypeStruct(candidates.shape, jnp.bfloat16),
        in_specs=[whole()] * (4 + len(arrays)),
        out_specs=whole(),
        compiler_params=PARAMS,
        name="finish",
    )(candidates, term, gate, w_out, *arrays)


def layer(history, candidates, hist_length, visible, w_proj, w_out):
    width = w_out.shape[0]
    size = lax.axis_size("hist")
    masks = []
    bit = size // 2
    while bit > 1:
        masks.append(bit | 1)
        bit //= 2
    rows = candidates.shape[0]
    first_op = spark()
    keys, self_key, rows_both = project_keys(history, candidates, w_proj, first_op)
    values, self_value = project_values(rows_both, w_proj, rows)
    other_keys = swapped(keys, "hist", 1)
    other_values = swapped(values, "hist", 1)
    got = swapped(candidates, "hist", masks[0])
    got_visible = swapped(visible, "hist", masks[0])
    inner = project_queries(candidates, got, visible, got_visible, hist_length, w_proj)
    for mask in masks[1:-2]:
        got = swapped(inner, "hist", mask)
        inner = join(inner, got)
    outer = swapped(inner, "hist", masks[-2])
    far_inner = swapped(inner, "hist", masks[-1])
    far_outer = swapped(outer, "hist", masks[-1])
    shards = (keys, values, other_keys, other_values)
    blocks = inner.shape[0] // rows
    sides = min(blocks, 2)
    sent_inner, *sent_outer = attend([far_inner, far_outer], shards, HEADS, (1, sides), True)
    got_outer = [None] * sides
    for side in reversed(range(sides)):
        got_outer[side] = swapped(sent_outer[side], "hist", masks[-1])
    got_inner = swapped(sent_inner, "hist", masks[-1])
    near_inner, near_outer = attend([inner, outer], shards, HEADS, (1, 1), False)
    gate, term = own(inner, rows_both, w_proj, self_key, self_value, HEADS)
    piece = blocks * rows // sides
    terms = [[(near_outer, side * piece), (got_outer[side], 0)] for side in range(sides)]
    last = []
    stage = len(masks) - 2
    while True:
        got = [None] * sides
        for side in reversed(range(sides)):
            sent = emit(terms[side], piece, width)
            got[side] = swapped(sent, "hist", masks[stage])
        last.append(got[0])
        if blocks == 1:
            break
        blocks //= 2
        sides = min(blocks, 2)
        piece = blocks * rows // sides
        terms = []
        for side in range(sides):
            first = blocks * rows + side * piece
            terms.append([(near_inner, first), (got_inner, first)])
            terms[-1] += [(array, first) for array in last[:-1]] + [(got[1], side * piece)]
        stage -= 1
    terms = [(near_inner, 0), (got_inner, 0)] + [(array, 0) for array in last]
    return finish(candidates, terms, term, gate, w_out)


def solution(mesh):
    in_specs = (
        P(("groups", "hist"), None),
        P(("groups", "hist"), None),
        P("groups"),
        P(("groups", "hist")),
        P(),
        P(),
    )
    out_specs = P(("groups", "hist"), None)
    return jax.shard_map(layer, mesh=mesh, in_specs=in_specs, out_specs=out_specs, check_vma=False)
```

```python
import jax
import jax.numpy as jnp
from jax import lax
from jax.experimental import pallas as pl
from jax.experimental.pallas import tpu as pltpu
from jax.sharding import PartitionSpec as P


HEADS = 8
EPS = 1e-06
EXTRA = 128
STEPS = 32000.0
GRANT = 8 * 1024 * 1024
PARAMS = pltpu.CompilerParams(vmem_limit_bytes=GRANT)


def swapped(shard, axis, mask):
    size = lax.axis_size(axis)
    return lax.ppermute(shard, axis, [(i, i ^ mask) for i in range(size)])


def norm(rows):
    centred = rows - jnp.mean(rows, axis=-1, keepdims=True)
    spread = jnp.mean(centred * centred, axis=-1, keepdims=True)
    return centred * lax.rsqrt(spread + EPS)


def silu(x):
    half = x * 0.5
    return half + half * jnp.tanh(half)


def whole():
    return pl.BlockSpec(memory_space=pltpu.VMEM)


def encode(rows, out_ref):
    count, width = rows.shape
    top = jnp.max(jnp.abs(rows), axis=-1, keepdims=True)
    exponent = jnp.ceil(jnp.log2(jnp.maximum(top, 1e-30)))
    code = jnp.round(rows * (STEPS * jnp.exp2(-exponent)))
    out_ref[:, :width] = code.astype(jnp.int32).astype(jnp.int16)
    out_ref[:, width:] = (
        jnp.broadcast_to(exponent, (count, EXTRA)).astype(jnp.int32).astype(jnp.int16)
    )


def decode(code, width):
    code = code.astype(jnp.int32).astype(jnp.float32)
    return code[:, :width] * (jnp.exp2(code[:, width : width + 1]) * (1 / STEPS))


def stay(array):
    return pltpu.with_memory_space_constraint(array, pltpu.HBM)


def near_by(*arrays):
    return [pltpu.with_memory_space_constraint(array, pltpu.VMEM) for array in arrays]


def hbm():
    return pl.BlockSpec(memory_space=pltpu.HBM)


def limits_of(packed, width):
    high = packed[:, width : width + 1].astype(jnp.float32)
    low = packed[:, width + 1 : width + 2].astype(jnp.float32)
    return high * 256 + low


def normed(rows):
    return norm(rows.astype(jnp.float32)).astype(jnp.bfloat16)


def in_halves(numbers):
    high = jnp.floor(numbers * (1 / 256))
    lane = lax.broadcasted_iota(jnp.int32, (numbers.shape[0], EXTRA), 1)
    return jnp.where(lane == 0, high, numbers - high * 256).astype(jnp.bfloat16)


def begin(candidates, visible):
    rows, width = candidates.shape

    def body(cand_ref, visible_ref, out_ref, offsets, sems):
        loads = [
            pltpu.make_async_copy(visible_ref, offsets, sems.at[0]),
            pltpu.make_async_copy(cand_ref, out_ref.at[:, pl.ds(0, width)], sems.at[1]),
        ]
        for load in loads:
            load.start()
        loads[0].wait()
        diagonal = lax.broadcasted_iota(jnp.int32, (rows, rows), 0) == lax.broadcasted_iota(
            jnp.int32, (rows, rows), 1
        )
        across = jnp.broadcast_to(offsets[...], (rows, rows)).astype(jnp.float32)
        down = jnp.sum(jnp.where(diagonal, across, 0.0), axis=1, keepdims=True)
        out_ref[:, width:] = in_halves(down)
        loads[1].wait()

    return pl.pallas_call(
        body,
        out_shape=jax.ShapeDtypeStruct((rows, width + EXTRA), jnp.bfloat16),
        in_specs=[hbm()] * 2,
        out_specs=whole(),
        scratch_shapes=[pltpu.VMEM((1, rows), jnp.int32), pltpu.SemaphoreType.DMA((2,))],
        compiler_params=PARAMS,
        cost_estimate=pl.CostEstimate(
            flops=6 * width**3, bytes_accessed=20 * width**2, transcendentals=0
        ),
        name="begin",
    )(stay(candidates), stay(visible.reshape(1, rows)))


def project(rows_ref, w_ref, first, tile, n_keys, out_ref, self_ref):
    width = out_ref.shape[1]
    for at in range(0, width, tile):
        made = silu(
            jnp.dot(
                rows_ref[...],
                w_ref[:, first + at : first + at + tile],
                preferred_element_type=jnp.float32,
            )
        ).astype(jnp.bfloat16)
        out_ref[:, at : at + tile] = made[:n_keys]
        self_ref[:, at : at + tile] = made[n_keys:]


def project_keys(history, packed, w_proj):
    n_keys, width = history.shape
    rows = packed.shape[0]
    tile = min(256, width)

    def body(hist_ref, packed_ref, w_ref, key_ref, self_ref, rows_ref):
        rows_ref[n_keys:] = normed(packed_ref[:, :width])
        rows_ref[:n_keys] = normed(hist_ref[...])
        project(rows_ref, w_ref, 2 * width, tile, n_keys, key_ref, self_ref)

    return pl.pallas_call(
        body,
        out_shape=(
            jax.ShapeDtypeStruct((n_keys, width), jnp.bfloat16),
            jax.ShapeDtypeStruct((rows, width), jnp.bfloat16),
            jax.ShapeDtypeStruct((n_keys + rows, width), jnp.bfloat16),
        ),
        in_specs=[whole()] * 3,
        out_specs=[whole()] * 3,
        compiler_params=PARAMS,
        name="keys",
    )(*near_by(history, packed, w_proj))


def project_values(rows_both, w_proj, rows):
    width = rows_both.shape[1]
    n_keys = rows_both.shape[0] - rows
    tile = min(256, width)

    def body(rows_ref, w_ref, value_ref, self_ref):
        project(rows_ref, w_ref, 3 * width, tile, n_keys, value_ref, self_ref)

    return pl.pallas_call(
        body,
        out_shape=(
            jax.ShapeDtypeStruct((n_keys, width), jnp.bfloat16),
            jax.ShapeDtypeStruct((rows, width), jnp.bfloat16),
        ),
        in_specs=[whole()] * 2,
        out_specs=[whole()] * 2,
        compiler_params=PARAMS,
        name="values",
    )(*near_by(rows_both, w_proj))


def project_queries(packed, got, hist_length, w_proj):
    rows = packed.shape[0]
    width = w_proj.shape[0]
    tile = min(256, width)

    def body(length_ref, packed_ref, got_ref, w_ref, out_ref):
        length = length_ref[0].astype(jnp.float32)
        for first, ref in ((0, packed_ref), (rows, got_ref)):
            limit = jnp.minimum(limits_of(ref[...], width), length)
            out_ref[first : first + rows, width:] = in_halves(limit)
        both = jnp.concatenate(
            [normed(packed_ref[:, :width]), normed(got_ref[:, :width])], axis=0
        )
        for at in range(0, width, tile):
            out_ref[:, at : at + tile] = silu(
                jnp.dot(
                    both,
                    w_ref[:, width + at : width + at + tile],
                    preferred_element_type=jnp.float32,
                )
            ).astype(jnp.bfloat16)

    return pl.pallas_call(
        body,
        out_shape=jax.ShapeDtypeStruct((2 * rows, width + EXTRA), jnp.bfloat16),
        in_specs=[pl.BlockSpec(memory_space=pltpu.SMEM)] + [whole()] * 3,
        out_specs=whole(),
        compiler_params=PARAMS,
        name="queries",
    )(hist_length, *near_by(packed, got, w_proj))


def join(first, second):
    rows = first.shape[0]

    def body(first_ref, second_ref, out_ref):
        out_ref[:rows] = first_ref[...]
        out_ref[rows:] = second_ref[...]

    return pl.pallas_call(
        body,
        out_shape=jax.ShapeDtypeStruct((2 * rows, first.shape[1]), first.dtype),
        in_specs=[whole()] * 2,
        out_specs=whole(),
        compiler_params=PARAMS,
        name="join",
    )(first, second)


def attend_kernel(heads, query, k0, v0, k1, v1, acc_ref):
    n_keys, width = k0.shape
    size = width // heads
    rows = query.shape[0]
    limit = limits_of(query, width)
    inverse = 1.0 / (limit + 1.0)
    position = lax.broadcasted_iota(jnp.int32, (rows, n_keys), 1).astype(jnp.float32)
    sides = ((k0, v0), (k1, v1))
    share = []
    for side in range(2):
        base = ((lax.axis_index("hist") ^ side) * n_keys).astype(jnp.float32)
        share.append(jnp.where(position + base < limit, inverse, 0.0))

    def scores_of(head):
        cols = slice(head * size, (head + 1) * size)
        return [
            lax.dot_general(
                query[:, cols],
                k[:, cols],
                (((1,), (1,)), ((), ())),
                preferred_element_type=jnp.float32,
            )
            for k, _ in sides
        ]

    ahead = scores_of(0)
    for head in range(heads):
        scores = ahead
        if head + 1 < heads:
            ahead = scores_of(head + 1)
        cols = slice(head * size, (head + 1) * size)
        total = None
        for side, (_, v) in enumerate(sides):
            half = scores[side] * (0.5 * size ** (-0.5))
            weight = ((half + half * jnp.tanh(half)) * share[side]).astype(jnp.bfloat16)
            part = jnp.dot(weight, v[:, cols], preferred_element_type=jnp.float32)
            total = part if total is None else total + part
        acc_ref[:, cols] = total
    made = acc_ref[...]
    return made - jnp.mean(made, axis=-1, keepdims=True)


def attend(queries, shards, heads, parts, coded):
    rows = queries[0].shape[0]
    _, width = shards[0].shape
    blocks = len(queries)
    pieces = [rows // part for part in parts for _ in range(part)]

    def body(*refs):
        ins, shard_refs, outs = refs[:blocks], refs[blocks : blocks + 4], refs[blocks + 4 : -1]
        query = jnp.concatenate([ref[...] for ref in ins], axis=0)
        made = attend_kernel(heads, query, *shard_refs, refs[-1])
        first = 0
        for piece, out_ref in zip(pieces, outs):
            part = made[first : first + piece]
            first += piece
            if coded:
                encode(part, out_ref)
            else:
                out_ref[...] = part

    return pl.pallas_call(
        body,
        out_shape=[
            jax.ShapeDtypeStruct((piece, width + EXTRA), jnp.int16)
            if coded
            else jax.ShapeDtypeStruct((piece, width), jnp.float32)
            for piece in pieces
        ],
        in_specs=[whole()] * (blocks + 4),
        out_specs=[whole()] * len(pieces),
        scratch_shapes=[pltpu.VMEM((blocks * rows, width), jnp.float32)],
        compiler_params=PARAMS,
    )(*near_by(*queries, *shards))


def own_kernel(heads, tile, query_ref, rows_ref, w_ref, key_ref, value_ref, gate_ref, term_ref):
    rows, width = key_ref.shape
    size = width // heads
    query = query_ref[:rows, :width].astype(jnp.float32)
    inverse = 1.0 / (limits_of(query_ref[:rows], width) + 1.0)
    products = query * key_ref[...].astype(jnp.float32)
    for head in range(heads):
        cols = slice(head * size, (head + 1) * size)
        score = jnp.sum(products[:, cols], axis=-1, keepdims=True)
        weight = (silu(score * size ** (-0.5)) * inverse).astype(jnp.bfloat16)
        term_ref[:, cols] = weight.astype(jnp.float32) * value_ref[:, cols].astype(jnp.float32)
    for at in range(0, width, tile):
        gate_ref[:, at : at + tile] = silu(
            jnp.dot(
                rows_ref[rows_ref.shape[0] - rows :],
                w_ref[:, at : at + tile],
                preferred_element_type=jnp.float32,
            )
        ).astype(jnp.bfloat16)


def own(query, rows_both, w_proj, self_key, self_value, heads):
    rows, width = self_key.shape
    tile = min(256, width)

    def body(*refs):
        own_kernel(heads, tile, *refs)

    return pl.pallas_call(
        body,
        out_shape=(
            jax.ShapeDtypeStruct((rows, width), jnp.bfloat16),
            jax.ShapeDtypeStruct((rows, width), jnp.float32),
        ),
        in_specs=[whole()] * 5,
        out_specs=[whole()] * 2,
        compiler_params=PARAMS,
        name="own",
    )(*near_by(query, rows_both, w_proj, self_key, self_value))


def total_of(terms, refs, rows, width):
    total = None
    for place, first in terms:
        part = refs[place][first : first + rows]
        if part.dtype == jnp.int16:
            part = decode(part, width)
        total = part if total is None else total + part
    return total


def placed(pieces):
    arrays = []
    lists = []
    for terms in pieces:
        listed = []
        for array, first in terms:
            place = next((i for i, seen in enumerate(arrays) if seen is array), None)
            if place is None:
                place = len(arrays)
                arrays.append(array)
            listed.append((place, first))
        lists.append(listed)
    return arrays, lists


def emit(terms, rows, width):
    arrays, (listed,) = placed([terms])

    def body(*refs):
        encode(total_of(listed, refs, rows, width), refs[-1])

    return pl.pallas_call(
        body,
        out_shape=jax.ShapeDtypeStruct((rows, width + EXTRA), jnp.int16),
        in_specs=[whole()] * len(arrays),
        out_specs=whole(),
        compiler_params=PARAMS,
        name="emit",
    )(*arrays)


def finish(candidates, terms, term, gate, w_out):
    arrays, (listed,) = placed([terms])

    def body(cand_ref, term_ref, gate_ref, w_ref, *refs):
        rows, width = cand_ref.shape
        attended = total_of(listed, refs, rows, width) + term_ref[...]
        mixed = (norm(attended) * gate_ref[...].astype(jnp.float32)).astype(jnp.bfloat16)
        refs[-1][...] = (
            cand_ref[...].astype(jnp.float32)
            + jnp.dot(mixed, w_ref[...], preferred_element_type=jnp.float32)
        ).astype(jnp.bfloat16)

    return pl.pallas_call(
        body,
        out_shape=jax.ShapeDtypeStruct(candidates.shape, jnp.bfloat16),
        in_specs=[whole()] * (4 + len(arrays)),
        out_specs=whole(),
        compiler_params=PARAMS,
        name="finish",
    )(candidates, term, gate, w_out, *arrays)


def layer(history, candidates, hist_length, visible, w_proj, w_out):
    width = w_out.shape[0]
    size = lax.axis_size("hist")
    masks = []
    bit = size // 2
    while bit > 1:
        masks.append(bit | 1)
        bit //= 2
    rows = candidates.shape[0]
    packed = begin(candidates, visible)
    keys, self_key, rows_both = project_keys(history, packed, w_proj)
    values, self_value = project_values(rows_both, w_proj, rows)
    other_keys = swapped(keys, "hist", 1)
    other_values = swapped(values, "hist", 1)
    got = swapped(packed, "hist", masks[0])
    inner = project_queries(packed, got, hist_length, w_proj)
    for mask in masks[1:-2]:
        got = swapped(inner, "hist", mask)
        inner = join(inner, got)
    outer = swapped(inner, "hist", masks[-2])
    far_inner = swapped(inner, "hist", masks[-1])
    far_outer = swapped(outer, "hist", masks[-1])
    shards = (keys, values, other_keys, other_values)
    blocks = inner.shape[0] // rows
    sides = min(blocks, 2)
    sent_inner, *sent_outer = attend([far_inner, far_outer], shards, HEADS, (1, sides), True)
    got_outer = [None] * sides
    for side in reversed(range(sides)):
        got_outer[side] = swapped(sent_outer[side], "hist", masks[-1])
    got_inner = swapped(sent_inner, "hist", masks[-1])
    near_inner, near_outer = attend([inner, outer], shards, HEADS, (1, 1), False)
    gate, term = own(inner, rows_both, w_proj, self_key, self_value, HEADS)
    piece = blocks * rows // sides
    terms = [[(near_outer, side * piece), (got_outer[side], 0)] for side in range(sides)]
    last = []
    stage = len(masks) - 2
    while True:
        got = [None] * sides
        for side in reversed(range(sides)):
            sent = emit(terms[side], piece, width)
            got[side] = swapped(sent, "hist", masks[stage])
        last.append(got[0])
        if blocks == 1:
            break
        blocks //= 2
        sides = min(blocks, 2)
        piece = blocks * rows // sides
        terms = []
        for side in range(sides):
            first = blocks * rows + side * piece
            terms.append([(near_inner, first), (got_inner, first)])
            terms[-1] += [(array, first) for array in last[:-1]] + [(got[1], side * piece)]
        stage -= 1
    terms = [(near_inner, 0), (got_inner, 0)] + [(array, 0) for array in last]
    return finish(candidates, terms, term, gate, w_out)


def solution(mesh):
    in_specs = (
        P(("groups", "hist"), None),
        P(("groups", "hist"), None),
        P("groups"),
        P(("groups", "hist")),
        P(),
        P(),
    )
    out_specs = P(("groups", "hist"), None)
    return jax.shard_map(layer, mesh=mesh, in_specs=in_specs, out_specs=out_specs, check_vma=False)
```

```python
import jax
import jax.numpy as jnp
from jax import lax
from jax.experimental import pallas as pl
from jax.experimental.pallas import tpu as pltpu
from jax.sharding import PartitionSpec as P


HEADS = 8
EPS = 1e-06
EXTRA = 128
STEPS = 32000.0
GRANT = 8 * 1024 * 1024
PARAMS = pltpu.CompilerParams(vmem_limit_bytes=GRANT)


def swapped(shard, axis, mask):
    size = lax.axis_size(axis)
    return lax.ppermute(shard, axis, [(i, i ^ mask) for i in range(size)])


def norm(rows):
    centred = rows - jnp.mean(rows, axis=-1, keepdims=True)
    spread = jnp.mean(centred * centred, axis=-1, keepdims=True)
    return centred * lax.rsqrt(spread + EPS)


def silu(x):
    half = x * 0.5
    return half + half * jnp.tanh(half)


def whole():
    return pl.BlockSpec(memory_space=pltpu.VMEM)


def encode(rows, out_ref):
    count, width = rows.shape
    top = jnp.max(jnp.abs(rows), axis=-1, keepdims=True)
    exponent = jnp.ceil(jnp.log2(jnp.maximum(top, 1e-30)))
    code = jnp.round(rows * (STEPS * jnp.exp2(-exponent)))
    out_ref[:, :width] = code.astype(jnp.int32).astype(jnp.int16)
    out_ref[:, width:] = (
        jnp.broadcast_to(exponent, (count, EXTRA)).astype(jnp.int32).astype(jnp.int16)
    )


def decode(code, width):
    code = code.astype(jnp.int32).astype(jnp.float32)
    return code[:, :width] * (jnp.exp2(code[:, width : width + 1]) * (1 / STEPS))


def stay(array):
    return pltpu.with_memory_space_constraint(array, pltpu.HBM)


def near_by(*arrays):
    return [pltpu.with_memory_space_constraint(array, pltpu.VMEM) for array in arrays]


def hbm():
    return pl.BlockSpec(memory_space=pltpu.HBM)


def limits_of(packed, width):
    high = packed[:, width : width + 1].astype(jnp.float32)
    low = packed[:, width + 1 : width + 2].astype(jnp.float32)
    return high * 256 + low


def normed(rows):
    return norm(rows.astype(jnp.float32)).astype(jnp.bfloat16)


def in_halves(numbers):
    high = jnp.floor(numbers * (1 / 256))
    lane = lax.broadcasted_iota(jnp.int32, (numbers.shape[0], EXTRA), 1)
    return jnp.where(lane == 0, high, numbers - high * 256).astype(jnp.bfloat16)


def begin(candidates, visible):
    rows, width = candidates.shape

    def body(cand_ref, visible_ref, out_ref, offsets, sems):
        loads = [
            pltpu.make_async_copy(visible_ref, offsets, sems.at[0]),
            pltpu.make_async_copy(cand_ref, out_ref.at[:, pl.ds(0, width)], sems.at[1]),
        ]
        for load in loads:
            load.start()
        loads[0].wait()
        diagonal = lax.broadcasted_iota(jnp.int32, (rows, rows), 0) == lax.broadcasted_iota(
            jnp.int32, (rows, rows), 1
        )
        across = jnp.broadcast_to(offsets[...], (rows, rows)).astype(jnp.float32)
        down = jnp.sum(jnp.where(diagonal, across, 0.0), axis=1, keepdims=True)
        out_ref[:, width:] = in_halves(down)
        loads[1].wait()

    return pl.pallas_call(
        body,
        out_shape=jax.ShapeDtypeStruct((rows, width + EXTRA), jnp.bfloat16),
        in_specs=[hbm()] * 2,
        out_specs=whole(),
        scratch_shapes=[pltpu.VMEM((1, rows), jnp.int32), pltpu.SemaphoreType.DMA((2,))],
        compiler_params=PARAMS,
        cost_estimate=pl.CostEstimate(
            flops=6 * width**3, bytes_accessed=20 * width**2, transcendentals=0
        ),
        name="begin",
    )(stay(candidates), stay(visible.reshape(1, rows)))


def project(rows_ref, w_ref, first, tile, n_keys, out_ref, self_ref):
    width = out_ref.shape[1]
    for at in range(0, width, tile):
        made = silu(
            jnp.dot(
                rows_ref[...],
                w_ref[:, first + at : first + at + tile],
                preferred_element_type=jnp.float32,
            )
        ).astype(jnp.bfloat16)
        out_ref[:, at : at + tile] = made[:n_keys]
        self_ref[:, at : at + tile] = made[n_keys:]


def project_keys(history, packed, w_proj):
    n_keys, width = history.shape
    rows = packed.shape[0]
    tile = min(256, width)

    def body(hist_ref, packed_ref, w_ref, key_ref, self_ref, rows_ref):
        rows_ref[n_keys:] = normed(packed_ref[:, :width])
        rows_ref[:n_keys] = normed(hist_ref[...])
        project(rows_ref, w_ref, 2 * width, tile, n_keys, key_ref, self_ref)

    return pl.pallas_call(
        body,
        out_shape=(
            jax.ShapeDtypeStruct((n_keys, width), jnp.bfloat16),
            jax.ShapeDtypeStruct((rows, width), jnp.bfloat16),
            jax.ShapeDtypeStruct((n_keys + rows, width), jnp.bfloat16),
        ),
        in_specs=[whole()] * 3,
        out_specs=[whole()] * 3,
        compiler_params=PARAMS,
        name="keys",
    )(*near_by(history, packed, w_proj))


def project_values(rows_both, w_proj, rows):
    width = rows_both.shape[1]
    n_keys = rows_both.shape[0] - rows
    tile = min(256, width)

    def body(rows_ref, w_ref, value_ref, self_ref):
        project(rows_ref, w_ref, 3 * width, tile, n_keys, value_ref, self_ref)

    return pl.pallas_call(
        body,
        out_shape=(
            jax.ShapeDtypeStruct((n_keys, width), jnp.bfloat16),
            jax.ShapeDtypeStruct((rows, width), jnp.bfloat16),
        ),
        in_specs=[whole()] * 2,
        out_specs=[whole()] * 2,
        compiler_params=PARAMS,
        name="values",
    )(*near_by(rows_both, w_proj))


def project_queries(packed, got, hist_length, w_proj):
    rows = packed.shape[0]
    width = w_proj.shape[0]
    tile = min(256, width)

    def body(length_ref, packed_ref, got_ref, w_ref, out_ref):
        length = length_ref[0].astype(jnp.float32)
        for first, ref in ((0, packed_ref), (rows, got_ref)):
            limit = jnp.minimum(limits_of(ref[...], width), length)
            out_ref[first : first + rows, width:] = in_halves(limit)
        both = jnp.concatenate(
            [normed(packed_ref[:, :width]), normed(got_ref[:, :width])], axis=0
        )
        for at in range(0, width, tile):
            out_ref[:, at : at + tile] = silu(
                jnp.dot(
                    both,
                    w_ref[:, width + at : width + at + tile],
                    preferred_element_type=jnp.float32,
                )
            ).astype(jnp.bfloat16)

    return pl.pallas_call(
        body,
        out_shape=jax.ShapeDtypeStruct((2 * rows, width + EXTRA), jnp.bfloat16),
        in_specs=[pl.BlockSpec(memory_space=pltpu.SMEM)] + [whole()] * 3,
        out_specs=whole(),
        compiler_params=PARAMS,
        name="queries",
    )(hist_length, *near_by(packed, got, w_proj))


def join(first, second):
    rows = first.shape[0]

    def body(first_ref, second_ref, out_ref):
        out_ref[:rows] = first_ref[...]
        out_ref[rows:] = second_ref[...]

    return pl.pallas_call(
        body,
        out_shape=jax.ShapeDtypeStruct((2 * rows, first.shape[1]), first.dtype),
        in_specs=[whole()] * 2,
        out_specs=whole(),
        compiler_params=PARAMS,
        name="join",
    )(first, second)


def attend_kernel(heads, query, sides, acc_ref, held_ref):
    n_keys, width = sides[0][0].shape
    size = width // heads
    rows = query.shape[0]
    limit = limits_of(query, width)
    inverse = 1.0 / (limit + 1.0)
    position = lax.broadcasted_iota(jnp.int32, (rows, n_keys), 1).astype(jnp.float32)
    share = []
    for _, _, twin in sides:
        base = ((lax.axis_index("hist") ^ twin) * n_keys).astype(jnp.float32)
        share.append(jnp.where(position + base < limit, inverse, 0.0))

    def scores_of(head):
        cols = slice(head * size, (head + 1) * size)
        return [
            lax.dot_general(
                query[:, cols],
                k[:, cols],
                (((1,), (1,)), ((), ())),
                preferred_element_type=jnp.float32,
            )
            for k, _, _ in sides
        ]

    ahead = scores_of(0)
    for head in range(heads):
        scores = ahead
        if head + 1 < heads:
            ahead = scores_of(head + 1)
        cols = slice(head * size, (head + 1) * size)
        total = None if held_ref is None else held_ref[:, cols]
        for place, (_, v, _) in enumerate(sides):
            half = scores[place] * (0.5 * size ** (-0.5))
            weight = ((half + half * jnp.tanh(half)) * share[place]).astype(jnp.bfloat16)
            part = jnp.dot(weight, v[:, cols], preferred_element_type=jnp.float32)
            total = part if total is None else total + part
        acc_ref[:, cols] = total


def attend(queries, shards, twins, heads, held, pieces):
    rows = queries[0].shape[0]
    _, width = shards[0].shape
    blocks, count = len(queries), len(shards)
    given = [] if held is None else [held]

    def body(*refs):
        ins, shard_refs = refs[:blocks], refs[blocks : blocks + count]
        held_ref = None if held is None else refs[blocks + count]
        outs = refs[blocks + count + len(given) :]
        acc_ref = outs[-1]
        query = jnp.concatenate([ref[...] for ref in ins], axis=0)
        sides = [(*shard_refs[2 * i : 2 * i + 2], twin) for i, twin in enumerate(twins)]
        attend_kernel(heads, query, sides, acc_ref, held_ref)
        if pieces:
            made = acc_ref[...]
            made = made - jnp.mean(made, axis=-1, keepdims=True)
        first = 0
        for (piece, coded), out_ref in zip(pieces, outs):
            part = made[first : first + piece]
            first += piece
            if coded:
                encode(part, out_ref)
            else:
                out_ref[...] = part

    whole_acc = jax.ShapeDtypeStruct((blocks * rows, width), jnp.float32)
    out = [
        jax.ShapeDtypeStruct((piece, width + EXTRA), jnp.int16)
        if coded
        else jax.ShapeDtypeStruct((piece, width), jnp.float32)
        for piece, coded in pieces
    ]
    return pl.pallas_call(
        body,
        out_shape=out or [whole_acc],
        in_specs=[whole()] * (blocks + count + len(given)),
        out_specs=[whole()] * (len(out) or 1),
        scratch_shapes=[pltpu.VMEM((blocks * rows, width), jnp.float32)] if out else [],
        compiler_params=PARAMS,
    )(*near_by(*queries, *shards, *given))


def own_kernel(heads, tile, query_ref, rows_ref, w_ref, key_ref, value_ref, gate_ref, term_ref):
    rows, width = key_ref.shape
    size = width // heads
    query = query_ref[:rows, :width].astype(jnp.float32)
    inverse = 1.0 / (limits_of(query_ref[:rows], width) + 1.0)
    products = query * key_ref[...].astype(jnp.float32)
    terms = []
    for head in range(heads):
        cols = slice(head * size, (head + 1) * size)
        score = jnp.sum(products[:, cols], axis=-1, keepdims=True)
        weight = (silu(score * size ** (-0.5)) * inverse).astype(jnp.bfloat16)
        terms.append(weight.astype(jnp.float32) * value_ref[:, cols].astype(jnp.float32))
    term = jnp.concatenate(terms, axis=1)
    term_ref[...] = term - jnp.mean(term, axis=-1, keepdims=True)
    for at in range(0, width, tile):
        gate_ref[:, at : at + tile] = silu(
            jnp.dot(
                rows_ref[rows_ref.shape[0] - rows :],
                w_ref[:, at : at + tile],
                preferred_element_type=jnp.float32,
            )
        ).astype(jnp.bfloat16)


def own(query, rows_both, w_proj, self_key, self_value, heads):
    rows, width = self_key.shape
    tile = min(256, width)

    def body(*refs):
        own_kernel(heads, tile, *refs)

    return pl.pallas_call(
        body,
        out_shape=(
            jax.ShapeDtypeStruct((rows, width), jnp.bfloat16),
            jax.ShapeDtypeStruct((rows, width), jnp.float32),
        ),
        in_specs=[whole()] * 5,
        out_specs=[whole()] * 2,
        compiler_params=PARAMS,
        name="own",
    )(*near_by(query, rows_both, w_proj, self_key, self_value))


def total_of(terms, refs, rows, width):
    total = None
    for place, first in terms:
        part = refs[place][first : first + rows]
        if part.dtype == jnp.int16:
            part = decode(part, width)
        total = part if total is None else total + part
    return total


def placed(pieces):
    arrays = []
    lists = []
    for terms in pieces:
        listed = []
        for array, first in terms:
            place = next((i for i, seen in enumerate(arrays) if seen is array), None)
            if place is None:
                place = len(arrays)
                arrays.append(array)
            listed.append((place, first))
        lists.append(listed)
    return arrays, lists


def emit(terms, rows, width):
    arrays, (listed,) = placed([terms])

    def body(*refs):
        encode(total_of(listed, refs, rows, width), refs[-1])

    return pl.pallas_call(
        body,
        out_shape=jax.ShapeDtypeStruct((rows, width + EXTRA), jnp.int16),
        in_specs=[whole()] * len(arrays),
        out_specs=whole(),
        compiler_params=PARAMS,
        name="emit",
    )(*arrays)


def gather_up(terms, term, width):
    arrays, (listed,) = placed([terms])
    rows = term.shape[0]

    def body(term_ref, *refs):
        refs[-1][...] = total_of(listed, refs, rows, width) + term_ref[...]

    return pl.pallas_call(
        body,
        out_shape=jax.ShapeDtypeStruct((rows, width), jnp.float32),
        in_specs=[whole()] * (1 + len(arrays)),
        out_specs=whole(),
        compiler_params=PARAMS,
        name="gather_up",
    )(term, *arrays)


def finish(candidates, held, got, gate, w_out):
    def body(cand_ref, held_ref, got_ref, gate_ref, w_ref, out_ref):
        width = cand_ref.shape[1]
        attended = held_ref[...] + decode(got_ref[...], width)
        mean = jnp.mean(attended, axis=-1, keepdims=True)
        square = jnp.mean(attended * attended, axis=-1, keepdims=True)
        scale = lax.rsqrt(jnp.maximum(square - mean * mean, 0.0) + EPS)
        normalised = (attended - mean) * scale
        mixed = (normalised * gate_ref[...].astype(jnp.float32)).astype(jnp.bfloat16)
        out_ref[...] = (
            cand_ref[...].astype(jnp.float32)
            + jnp.dot(mixed, w_ref[...], preferred_element_type=jnp.float32)
        ).astype(jnp.bfloat16)

    return pl.pallas_call(
        body,
        out_shape=jax.ShapeDtypeStruct(candidates.shape, jnp.bfloat16),
        in_specs=[whole()] * 5,
        out_specs=whole(),
        compiler_params=PARAMS,
        name="finish",
    )(candidates, held, got, gate, w_out)


def layer(history, candidates, hist_length, visible, w_proj, w_out):
    width = w_out.shape[0]
    size = lax.axis_size("hist")
    masks = []
    bit = size // 2
    while bit > 1:
        masks.append(bit | 1)
        bit //= 2
    rows = candidates.shape[0]
    packed = begin(candidates, visible)
    keys, self_key, rows_both = project_keys(history, packed, w_proj)
    values, self_value = project_values(rows_both, w_proj, rows)
    other_keys = swapped(keys, "hist", 1)
    other_values = swapped(values, "hist", 1)
    got = swapped(packed, "hist", masks[0])
    inner = project_queries(packed, got, hist_length, w_proj)
    for mask in masks[1:-2]:
        got = swapped(inner, "hist", mask)
        inner = join(inner, got)
    outer = swapped(inner, "hist", masks[-2])
    far_inner = swapped(inner, "hist", masks[-1])
    far_outer = swapped(outer, "hist", masks[-1])
    shards = (keys, values, other_keys, other_values)
    blocks = inner.shape[0] // rows
    sides = min(blocks, 2)
    count = blocks * rows
    early = [far_inner, inner, outer]
    (held,) = attend(early, (keys, values), (0,), HEADS, None, ())
    sent_inner, near_inner, near_outer = attend(
        early,
        (other_keys, other_values),
        (1,),
        HEADS,
        held,
        ((count, True), (count, False), (count, False)),
    )
    sent_outer = attend([far_outer], shards, (0, 1), HEADS, None, ((count // sides, True),) * sides)
    got_outer = [None] * sides
    for side in reversed(range(sides)):
        got_outer[side] = swapped(sent_outer[side], "hist", masks[-1])
    got_inner = swapped(sent_inner, "hist", masks[-1])
    gate, term = own(inner, rows_both, w_proj, self_key, self_value, HEADS)
    piece = blocks * rows // sides
    terms = [[(near_outer, side * piece), (got_outer[side], 0)] for side in range(sides)]
    last = []
    stage = len(masks) - 2
    while True:
        got = [None] * sides
        for side in reversed(range(sides)):
            sent = emit(terms[side], piece, width)
            got[side] = swapped(sent, "hist", masks[stage])
        last.append(got[0])
        if blocks == 1:
            break
        blocks //= 2
        sides = min(blocks, 2)
        piece = blocks * rows // sides
        terms = []
        for side in range(sides):
            first = blocks * rows + side * piece
            terms.append([(near_inner, first), (got_inner, first)])
            terms[-1] += [(array, first) for array in last[:-1]] + [(got[1], side * piece)]
        stage -= 1
    terms = [(near_inner, 0), (got_inner, 0)] + [(array, 0) for array in last[:-1]]
    held = gather_up(terms, term, width)
    return finish(candidates, held, last[-1], gate, w_out)


def solution(mesh):
    in_specs = (
        P(("groups", "hist"), None),
        P(("groups", "hist"), None),
        P("groups"),
        P(("groups", "hist")),
        P(),
        P(),
    )
    out_specs = P(("groups", "hist"), None)
    return jax.shard_map(layer, mesh=mesh, in_specs=in_specs, out_specs=out_specs, check_vma=False)
```
